512 devices in a mesh: replica: 16 (over y_lo, z), fsdp: 32 (over y_hi, x, core).
Axes of the slice: x: 4, y: 8 (y_hi: 4, y_lo: 2; y = y_hi * 2 + y_lo), z: 8, core: 2. Of those that a mesh axis runs over, the one named last changes fastest.
Arguments:
- node_feats: bfloat16 [65536, 1024], P(('replica', 'fsdp')), may hold values from -6 to 6
- neighbor_src: int32 [12, 65536], P(None, ('replica', 'fsdp')), may hold values from 0 to 4095, as said below
- distances: float32 [12, 65536], P(None, ('replica', 'fsdp')), may hold values from 0.8 to 5
- graph_ids: int32 [16, 4096], P('replica', 'fsdp'), may hold values from 0 to 7, never falling along the last dimension, each value on 1 to 1024 neighbouring positions
- msg_weight: bfloat16 [1024, 1024], P('fsdp'), may hold values from -0.1875 to 0.1875
- out_weight: bfloat16 [1024, 1024], P('fsdp'), may hold values from -0.1875 to 0.1875
- radial_weight: float32 [8, 1024], replicated, may hold values from -6 to 6
- cotangent: bfloat16 [65536, 1024], P(('replica', 'fsdp')), may hold values from -6 to 6
- fragment: int32 [1], replicated, may hold values from 0 to 7
Outputs:
- node_out: bfloat16 [65536, 1024], P(('replica', 'fsdp'))
- grad_msg: bfloat16 [16, 1024, 1024], P('replica', 'fsdp')
- grad_out: bfloat16 [16, 1024, 1024], P('replica', 'fsdp')
- outer_sum: float32 [2, 1024, 128], P(None, 'fsdp')
The draws below stay inside these ranges and needn't reach their ends.
Inputs may be any that keep to these rules, and one draw needn't show every extreme that they name: `neighbor_src`: each neighbour index lies within 32 positions of its own atom's index in the group, never equal to it, and inside the group. `graph_ids`: within each group the graph numbers never fall and every graph has at least one atom.
All inputs are finite; a program needn't handle non-finite values. Where the reference program divides by a largest or mean magnitude, that divisor is 1e-20 or more.
Results may differ from the reference program's by a relative error of at most 0.02.
Values may be sent and summed in bfloat16 or wider, within the bound.
A program may use at most 64 MiB of HBM per device.

```python
import math
import jax
import jax.numpy as jnp
import numpy as np
from jax import lax

CHANNELS = 1024
BASIS = 8
NEIGHBORS = 12
FRAG = 128
GRAPHS = 8
A_DEV = 128
HALO = 32
GROUP_ATOMS = 4096
ATOMS = 65536
N_REPLICA = 16
N_FSDP = 32


def draw_neighbor_src(key, part):
    first_key = jax.random.fold_in(key, 11)
    second_key = jax.random.fold_in(key, 23)
    position = jnp.arange(ATOMS, dtype=jnp.int32) % GROUP_ATOMS
    magnitude = jax.random.randint(first_key, (NEIGHBORS, ATOMS), 1, HALO + 1, dtype=jnp.int32)
    direction = jax.random.randint(second_key, (NEIGHBORS, ATOMS), 0, 2, dtype=jnp.int32) * 2 - 1
    offset = magnitude * direction
    candidate = position[None, :] + offset
    outside = (candidate < 0) | (candidate >= GROUP_ATOMS)
    return jnp.where(outside, position[None, :] - offset, candidate).astype(jnp.int32)


def level_of(own_key, dims, cuts, least, top_value):
    loudness, own = 1.0, jax.random.fold_in(own_key, 6)
    for dim, shards_of in cuts:
        heights = jnp.exp(jax.random.uniform(jax.random.fold_in(own, dim), (shards_of,), jnp.float32, least / len(cuts), top_value / len(cuts)))
        loudness = loudness * jnp.repeat(heights, dims[dim] // shards_of).reshape([-1 if axis == dim else 1 for axis in range(len(dims))])
    return loudness


def split_up(count, total, reach, lean):
    weights = [(1 << 20) // math.isqrt(grade ** lean) + 1 for grade in range(2, count + 1)]
    surplus, holding = total - reach - (count - 1), [1] * (count - 1)
    while surplus > 0:
        candidates = [i for i in range(count - 1) if holding[i] < reach]
        pool, left = sum([weights[i] for i in candidates]), surplus
        for i in candidates:
            more = min(reach - holding[i], max(1, left * weights[i] // pool), surplus)
            holding[i] = holding[i] + more
            surplus = surplus - more
    return np.array([reach] + holding)


def uneven_parts(own_key, count, total, reach, slope):
    if count == 2:
        one = jax.random.randint(own_key, (), max(1, total - reach), min(reach, total - 1) + 1)
        return jnp.stack([one, total - one])
    sizes = jnp.asarray(split_up(count, total, reach, slope), jnp.int32)
    twos = (count - 1) // 2
    source_of, receiver = sizes[1:1 + 2 * twos:2], sizes[2:2 + 2 * twos:2]
    room = jnp.minimum(source_of - 1, reach - receiver)
    moved = jax.random.randint(jax.random.fold_in(own_key, 1), (twos,), 0, 1 << 20) % (room + 1)
    sizes = sizes.at[1:1 + 2 * twos:2].set(source_of - moved).at[2:2 + 2 * twos:2].set(receiver + moved)
    return sizes[jax.random.permutation(jax.random.fold_in(own_key, 2), count)]


def bell_draw(stream_key, shape, scale, limit, cuts=(), held_as=jnp.bfloat16):
    level = level_of(stream_key, shape, cuts, -0.22, 0.18) if cuts else 1.0
    entries = jax.random.normal(stream_key, shape, jnp.float32) * scale * level
    return jnp.minimum(jnp.maximum(entries, -limit), limit).astype(held_as)


def setup_inputs(seed: int = 0) -> dict:
    key_of = jax.random.split(jax.random.key(seed), 10)
    node_feats = bell_draw(key_of[0], (ATOMS, CHANNELS), 1.0, 6.0, ((0, 512),))
    neighbor_src = draw_neighbor_src(jax.random.fold_in(key_of[9], 71), 0)
    distances = jnp.clip(0.8 + 4.2 * jax.random.uniform(key_of[2], (NEIGHBORS, ATOMS), jnp.float32) ** level_of(key_of[2], (NEIGHBORS, ATOMS), ((1, 512),), -0.2, 0.2), 0.8, 5.0)
    graph_ids = jax.vmap(lambda own: jnp.searchsorted(jnp.cumsum(uneven_parts(own, GRAPHS, GROUP_ATOMS, GROUP_ATOMS // 4, 2)), jnp.arange(GROUP_ATOMS), side="right"))(jax.random.split(key_of[3], N_REPLICA)).reshape((N_REPLICA, GROUP_ATOMS)).astype(jnp.int32)
    msg_weight = bell_draw(key_of[4], (CHANNELS, CHANNELS), CHANNELS ** -0.5, 0.1875, ((0, 32),))
    out_weight = bell_draw(key_of[5], (CHANNELS, CHANNELS), CHANNELS ** -0.5, 0.1875, ((0, 32),))
    radial_weight = bell_draw(key_of[6], (BASIS, CHANNELS), 1.0, 6.0, (), jnp.float32)
    cotangent = bell_draw(key_of[7], (ATOMS, CHANNELS), 1.0, 6.0, ((0, 512),))
    fragment = jax.random.randint(key_of[8], (1,), 0, CHANNELS // FRAG).astype(jnp.int32)
    return dict(node_feats=node_feats, neighbor_src=neighbor_src, distances=distances, graph_ids=graph_ids, msg_weight=msg_weight, out_weight=out_weight, radial_weight=radial_weight, cotangent=cotangent, fragment=fragment)


cutoff = 5.0
sharpness = 2.0
tiny = 1e-06

def radial(dist_row, radial_weight):
    basis_count = radial_weight.shape[0]
    centers = cutoff * jnp.arange(basis_count).astype(jnp.float32) / (basis_count - 1)
    envelope = 0.5 * (jnp.cos(jnp.pi * dist_row / cutoff) + 1.0)
    basis = jnp.exp(-sharpness * (dist_row[:, None] - centers[None, :]) ** 2) * envelope[:, None]
    return jnp.dot(basis, radial_weight, precision=lax.Precision.HIGHEST, preferred_element_type=jnp.float32)

def block_grads(left, right):
    left_blocks = left.reshape(N_FSDP, A_DEV, left.shape[1])
    right_blocks = right.reshape(N_FSDP, A_DEV, right.shape[1])

    def step(total, pair):
        partial_sum = lax.dot_general(pair[0], pair[1], (((0,), (0,)), ((), ())), preferred_element_type=jnp.float32)
        rounded = lax.optimization_barrier(partial_sum.astype(jnp.bfloat16))
        return (total + rounded.astype(jnp.float32), None)
    start_total = jnp.zeros((left.shape[1], right.shape[1]), jnp.float32)
    total, _ = lax.scan(step, start_total, (left_blocks, right_blocks))
    return total

def reference(node_feats, neighbor_src, distances, graph_ids, msg_weight, out_weight, radial_weight, cotangent, fragment):
    width = node_feats.shape[1]
    norm = 1.0 / math.sqrt(NEIGHBORS)
    feats_all = node_feats.reshape(N_REPLICA, GROUP_ATOMS, width)
    cot_all = cotangent.reshape(N_REPLICA, GROUP_ATOMS, width)
    src_all = jnp.transpose(neighbor_src.reshape(NEIGHBORS, N_REPLICA, GROUP_ATOMS), (1, 0, 2))
    dist_all = jnp.transpose(distances.reshape(NEIGHBORS, N_REPLICA, GROUP_ATOMS), (1, 0, 2))
    column = (fragment[0] * FRAG).astype(jnp.int32)

    def one_group(inputs):
        feats, src, dist, ids, cot = inputs
        projected = jnp.dot(feats, msg_weight, preferred_element_type=jnp.float32).astype(jnp.bfloat16)

        def gather_step(k, acc):
            rows = jnp.take(projected, src[k], axis=0).astype(jnp.float32)
            return acc + radial(dist[k], radial_weight) * rows
        agg = lax.fori_loop(0, NEIGHBORS, gather_step, jnp.zeros((GROUP_ATOMS, width), jnp.float32)) * norm
        act = jax.nn.silu(agg).astype(jnp.bfloat16)
        node_out = (feats.astype(jnp.float32) + jnp.dot(act, out_weight, preferred_element_type=jnp.float32)).astype(jnp.bfloat16)
        onehot = (ids[:, None] == jnp.arange(GRAPHS, dtype=jnp.int32)[None, :]).astype(jnp.float32)
        count = lax.optimization_barrier(jnp.sum(onehot, axis=0))
        weight = lax.optimization_barrier(jnp.sum(onehot * lax.rsqrt(count)[None, :], axis=1))
        dout = (weight[:, None] * cot.astype(jnp.float32)).astype(jnp.bfloat16)
        out_sum = block_grads(act, dout)
        dact = lax.dot_general(dout, out_weight, (((1,), (1,)), ((), ())), preferred_element_type=jnp.float32)
        sig = jax.nn.sigmoid(agg)
        dagg = dact * sig * (1.0 + agg * (1.0 - sig))

        def spread_step(k, acc):
            return acc.at[src[k]].add(radial(dist[k], radial_weight) * dagg * norm)
        dproj = lax.fori_loop(0, NEIGHBORS, spread_step, jnp.zeros((GROUP_ATOMS, width), jnp.float32)).astype(jnp.bfloat16)
        msg_sum = block_grads(feats, dproj)
        pieces = jnp.stack([lax.dynamic_slice_in_dim(msg_sum, column, FRAG, 1), lax.dynamic_slice_in_dim(out_sum, column, FRAG, 1)])
        scale = (lax.optimization_barrier(jnp.max(jnp.abs(pieces), axis=-1, keepdims=True)) + tiny).astype(jnp.bfloat16)
        code = (pieces / scale.astype(jnp.float32)).astype(jnp.bfloat16)
        terms = scale.astype(jnp.float32) * code.astype(jnp.float32)
        return (node_out, msg_sum.astype(jnp.bfloat16), out_sum.astype(jnp.bfloat16), terms)
    node_out, grad_msg, grad_out, terms = lax.map(one_group, (feats_all, src_all, dist_all, graph_ids, cot_all))
    return (node_out.reshape(N_REPLICA * GROUP_ATOMS, width), grad_msg, grad_out, lax.optimization_barrier(jnp.sum(terms, axis=0)))
```

```python
import functools
import math

import jax
import jax.numpy as jnp
from jax import lax
from jax.experimental import pallas as pl
from jax.experimental.pallas import tpu as pltpu
from jax.sharding import PartitionSpec as P

MESH = pl.DeviceIdType.MESH
F32 = jnp.float32
BF16 = jnp.bfloat16
GRAPHS = 8
FRAG = 128
A = 128
C = 1024
HC = 512
H = 32
NB = 12
BASIS = 8
W = 2 * A - 64
EXT = 2 * A + 2 * H
TINY = 1e-6


def contract(a, b, da, db):
    return lax.dot_general(a, b, (((da,), (db,)), ((), ())), preferred_element_type=F32)


def body(
    feats, src, dist, ids, wm, wo, radial, cot, frag,
    node_o, gmsg_o, gout_o, outer_o,
    wmb, wob, idb, fx, cotb, srcb, distb, part_r,
    rim_lo, rim_hi, xo, xm, yo, ym, oo, om,
    bas, mtv, mtc, mc, ps, act, dsl, act_t, feats_t, dout, rr, spread, dproj,
    part_s, rim_s, so, ko, sm, km, syo, sym, gf, tb,
    loc, s_wy, r_wy, s_iy, r_iy, s_oy, r_oy, s_wx, r_wx, s_ix, r_ix, s_ox, r_ox,
    s_misc, r_misc, s_xo, r_xo, s_xm, r_xm, s_yo, r_yo, s_ym, r_ym, s_oo, r_oo, s_om, r_om,
):
    r = lax.axis_index("replica")
    f = lax.axis_index("fsdp")
    ylo, z = r // 8, r % 8
    h, x, c = f // 8, (f // 2) % 4, f % 2
    q = f // 2
    s = 2 * ylo - 1
    xp, xn, x2 = (x + 1) % 4, (x + 3) % 4, (x + 2) % 4
    ha, hb, h2 = (h + s + 4) % 4, (h - s + 4) % 4, (h + 2) % 4
    half = h // 2

    def dev(ylo_, h_, x_, c_):
        return (ylo_ * 8 + z, h_ * 8 + x_ * 2 + c_)

    def chip(q_, c_):
        return (r, q_ * 2 + c_)

    partner = dev(ylo, h, x, 1 - c)
    right, left = dev(ylo, h, xp, c), dev(ylo, h, xn, c)
    qn, qp = (q + 1) % 16, (q + 15) % 16
    y_to = ((1 - ylo, ha), (ylo, ha), (1 - ylo, h2))
    y_in = (ha, hb, h2)
    y_from = ((1 - ylo, ha), (ylo, hb), (1 - ylo, h2))

    def send(a_, b_, ss, rs, to):
        cp = pltpu.make_async_remote_copy(
            src_ref=a_, dst_ref=b_, send_sem=ss, recv_sem=rs, device_id=to, device_id_type=MESH
        )
        cp.start()
        return cp

    def arrived(b_, ss, rs, frm):
        pltpu.make_async_remote_copy(
            src_ref=b_, dst_ref=b_, send_sem=ss, recv_sem=rs, device_id=frm, device_id_type=MESH
        ).wait_recv()

    bar = pltpu.get_barrier_semaphore()
    greet = [partner, right, left]
    for c_ in (0, 1):
        greet += [
            dev(ylo, ha, x, c_), dev(ylo, hb, x, c_), dev(ylo, h2, x, c_),
            dev(1 - ylo, ha, x, c_), dev(1 - ylo, h2, x, c_), chip(qn, c_), chip(qp, c_),
        ]
    greet += [((r + d) % 16, f) for d in range(1, 16)]
    for g in greet:
        pl.semaphore_signal(bar, inc=1, device_id=g, device_id_type=MESH)

    own = [
        pltpu.make_async_copy(
            wm.at[:, pl.ds(pl.multiple_of(c * HC, HC), HC)], wmb.at[h, x, c], loc.at[0]
        ),
        pltpu.make_async_copy(ids, idb.at[h, x, c], loc.at[1]),
        pltpu.make_async_copy(
            feats, fx.at[pl.ds(pl.multiple_of(H + A * c, H), A)], loc.at[2]
        ),
        pltpu.make_async_copy(cot, cotb.at[c], loc.at[3]),
        pltpu.make_async_copy(src, srcb.at[c], loc.at[4]),
        pltpu.make_async_copy(dist, distb.at[c], loc.at[5]),
    ]
    for o in own:
        o.start()

    @pl.when(half == c)
    def _():
        cp = pltpu.make_async_copy(wo, wob.at[h % 2, x, c], loc.at[6])
        cp.start()
        cp.wait()

    @pl.when(q == 0)
    def _():
        fx[0:H, :] = jnp.zeros((H, C), BF16)
        rim_lo[...] = jnp.zeros((H, HC), BF16)

    @pl.when(q == 15)
    def _():
        fx[H + 2 * A :, :] = jnp.zeros((H, C), BF16)
        rim_hi[...] = jnp.zeros((H, HC), BF16)

    for o in own:
        o.wait()
    pl.semaphore_wait(bar, len(greet))

    sent = []
    other = pl.ds(pl.multiple_of((1 - c) * HC, HC), HC)
    mine_c = pl.ds(pl.multiple_of(c * HC, HC), HC)
    sent.append(send(wm.at[:, other], wmb.at[h, x, c], s_wy.at[6], r_wy.at[6], partner))
    sent.append(send(ids, idb.at[h, x, c], s_iy.at[6], r_iy.at[6], partner))
    for j, (yl, hh) in enumerate(y_to):
        for c_ in (0, 1):
            to = dev(yl, hh, x, c_)
            sent.append(
                send(
                    wm.at[:, pl.ds(c_ * HC, HC)], wmb.at[h, x, c],
                    s_wy.at[2 * j + c_], r_wy.at[2 * j + c], to,
                )
            )
    for j, hh in enumerate((hb, ha, h2)):
        for c_ in (0, 1):
            sent.append(
                send(
                    ids, idb.at[h, x, c], s_iy.at[2 * j + c_], r_iy.at[2 * j + c],
                    dev(ylo, hh, x, c_),
                )
            )
    sent.append(send(src, srcb.at[c], s_misc.at[0], r_misc.at[0], partner))
    sent.append(send(dist, distb.at[c], s_misc.at[1], r_misc.at[1], partner))
    f_rows = pl.ds(pl.multiple_of(H + A * c, H), A)
    sent.append(send(feats, fx.at[f_rows], s_misc.at[2], r_misc.at[2], partner))
    sent.append(send(cot, cotb.at[c], s_misc.at[3], r_misc.at[3], partner))

    up_ok = jnp.logical_and(c == 1, q < 15)
    dn_ok = jnp.logical_and(c == 0, q > 0)

    def up_copy(c_):
        return pltpu.make_async_remote_copy(
            src_ref=feats.at[pl.ds(A - H, H)], dst_ref=fx.at[pl.ds(0, H)],
            send_sem=s_misc.at[4 + c_], recv_sem=r_misc.at[4],
            device_id=chip(qn, c_), device_id_type=MESH,
        )

    def dn_copy(c_):
        return pltpu.make_async_remote_copy(
            src_ref=feats.at[pl.ds(0, H)], dst_ref=fx.at[pl.ds(H + 2 * A, H)],
            send_sem=s_misc.at[4 + c_], recv_sem=r_misc.at[5],
            device_id=chip(qp, c_), device_id_type=MESH,
        )

    @pl.when(up_ok)
    def _():
        for c_ in (0, 1):
            up_copy(c_).start()

    @pl.when(dn_ok)
    def _():
        for c_ in (0, 1):
            dn_copy(c_).start()

    for j, (yl, hh) in enumerate(y_to):
        sent.append(
            send(
                wo, wob.at[h % 2, x, c], s_oy.at[j], r_oy.at[2 * j + c], dev(yl, hh, x, half)
            )
        )

    def wo_partner():
        return pltpu.make_async_remote_copy(
            src_ref=wo, dst_ref=wob.at[h % 2, x, c], send_sem=s_oy.at[3], recv_sem=r_oy.at[6],
            device_id=partner, device_id_type=MESH,
        )

    @pl.when(half != c)
    def _():
        wo_partner().start()

    def wm_forward(k):
        yb = h if k == 0 else y_in[k - 1]
        if k == 0:
            arrived(wmb.at[h, x, 1 - c], s_wy.at[6], r_wy.at[6], partner)
            arrived(idb.at[h, x, 1 - c], s_iy.at[6], r_iy.at[6], partner)
        else:
            for c_ in (0, 1):
                frm = dev(*y_from[k - 1], x, c_)
                i = 2 * (k - 1) + c_
                arrived(wmb.at[yb, x, c_], s_wy.at[i], r_wy.at[i], frm)
                arrived(idb.at[yb, x, c_], s_iy.at[i], r_iy.at[i], dev(ylo, yb, x, c_))
        for i, to in enumerate((right, left)):
            sent.append(send(wmb.at[yb, x], wmb.at[yb, x], s_wx.at[k, i], r_wx.at[k, i], to))
            sent.append(send(idb.at[yb, x], idb.at[yb, x], s_ix.at[k, i], r_ix.at[k, i], to))

    def wm_relay(k):
        yb = h if k == 0 else y_in[k - 1]
        arrived(wmb.at[yb, xn], s_wx.at[k, 0], r_wx.at[k, 0], left)
        arrived(idb.at[yb, xn], s_ix.at[k, 0], r_ix.at[k, 0], left)
        if k % 2:
            arrived(wmb.at[yb, xp], s_wx.at[k, 1], r_wx.at[k, 1], right)
            arrived(idb.at[yb, xp], s_ix.at[k, 1], r_ix.at[k, 1], right)
        xs, to = (xp, left) if k % 2 else (xn, right)
        sent.append(send(wmb.at[yb, xs], wmb.at[yb, xs], s_wx.at[k, 2], r_wx.at[k, 2], to))
        sent.append(send(idb.at[yb, xs], idb.at[yb, xs], s_ix.at[k, 2], r_ix.at[k, 2], to))

    def wm_finish(k):
        yb = h if k == 0 else y_in[k - 1]
        frm = right if k % 2 else left
        if not k % 2:
            arrived(wmb.at[yb, xp], s_wx.at[k, 1], r_wx.at[k, 1], right)
            arrived(idb.at[yb, xp], s_ix.at[k, 1], r_ix.at[k, 1], right)
        arrived(wmb.at[yb, x2], s_wx.at[k, 2], r_wx.at[k, 2], frm)
        arrived(idb.at[yb, x2], s_ix.at[k, 2], r_ix.at[k, 2], frm)

    norm = 1.0 / math.sqrt(NB)

    def build(p):
        d = distb[p]
        env = 0.5 * (jnp.cos(d * (math.pi / 5.0)) + 1.0) * norm
        for b in range(BASIS):
            bas[b] = jnp.exp(-2.0 * (d - 5.0 * b / (BASIS - 1)) ** 2) * env
        base = 2 * A * q - H + A * p

        def tile(t, carry):
            row = pl.multiple_of(t * 16, 16)
            at = row + base + lax.broadcasted_iota(jnp.int32, (16, A), 0)
            accs = [jnp.zeros((16, A), F32) for _ in range(BASIS)]
            for k in range(NB):
                hit = srcb[p, k : k + 1, :] == at
                for b in range(BASIS):
                    accs[b] = accs[b] + jnp.where(hit, bas[b, k : k + 1, :], 0.0)
            for b in range(BASIS):
                mtv[pl.ds(pl.multiple_of(b * W + row, 16), 16), :] = accs[b]
                mtc[p, pl.ds(row, 16), b * A : (b + 1) * A] = accs[b].astype(BF16)
            return carry

        lax.fori_loop(0, W // 16, tile, 0)
        for t in range(BASIS * W // A):
            mc[p, :, t * A : (t + 1) * A] = mtv[t * A : (t + 1) * A, :].T.astype(BF16)

    wm_forward(0)
    arrived(srcb.at[1 - c], s_misc.at[0], r_misc.at[0], partner)
    arrived(distb.at[1 - c], s_misc.at[1], r_misc.at[1], partner)
    build(0)
    wm_forward(1)
    wm_forward(2)
    wm_relay(0)
    build(1)
    wm_forward(3)
    wm_relay(1)
    wm_relay(2)

    for k in range(3):
        @pl.when(y_in[k] // 2 == c)
        def _(k=k):
            for c_ in (0, 1):
                i = 2 * k + c_
                arrived(
                    wob.at[y_in[k] % 2, x, c_], s_oy.at[0], r_oy.at[i], dev(*y_from[k], x, c_)
                )

    @pl.when(half == c)
    def _():
        arrived(wob.at[h % 2, x, 1 - c], s_oy.at[3], r_oy.at[6], partner)

    for e in (0, 1):
        for i, to in enumerate((right, left)):
            sent.append(send(wob.at[e, x], wob.at[e, x], s_ox.at[e, i], r_ox.at[e, i], to))
    wm_relay(3)

    arrived(fx.at[pl.ds(pl.multiple_of(H + A * (1 - c), H), A)], s_misc.at[2], r_misc.at[2], partner)
    for p in (0, 1):
        feats_t[:, :, :, p * A : (p + 1) * A] = (
            fx[H + p * A : H + (p + 1) * A, :].T.reshape(4, 4, 64, A)
        )
    arrived(cotb.at[1 - c], s_misc.at[3], r_misc.at[3], partner)

    @pl.when(q > 0)
    def _():
        arrived(fx.at[pl.ds(0, H)], s_misc.at[4], r_misc.at[4], chip(qp, 1))

    @pl.when(q < 15)
    def _():
        arrived(fx.at[pl.ds(H + 2 * A, H)], s_misc.at[4], r_misc.at[5], chip(qn, 0))

    for k in range(4):
        wm_finish(k)

    all_ids = idb[...].reshape(32, A)
    for p in (0, 1):
        mine = idb[h, x, p]
        wrow = jnp.zeros((1, A), F32)
        for g in range(GRAPHS):
            count = jnp.sum((all_ids == g).astype(F32), axis=0, keepdims=True)
            count = jnp.sum(count, axis=1, keepdims=True)
            wrow = wrow + jnp.where(mine == g, lax.rsqrt(jnp.broadcast_to(count, (1, A))), 0.0)
        wcol = jnp.broadcast_to(wrow, (A, A)).T
        for t in range(C // A):
            cols = slice(t * A, (t + 1) * A)
            dout[p * A : (p + 1) * A, cols] = (cotb[p, :, cols].astype(F32) * wcol).astype(BF16)

    wmat = wmb[...].reshape(C, HC)
    proj = jnp.dot(fx[...], wmat, preferred_element_type=F32).astype(BF16)
    spread[...] = proj.astype(F32)
    for p in (0, 1):
        for b in range(BASIS):
            ps[b * W : (b + 1) * W, :] = (
                spread[p * A : p * A + W, :] * radial[b : b + 1, mine_c]
            ).astype(BF16)
        agg = jnp.dot(mc[p], ps[...], preferred_element_type=F32)
        sig = 1.0 / (1.0 + jnp.exp(-agg))
        a16 = (agg * sig).astype(BF16)
        rows = slice(p * A, (p + 1) * A)
        act[rows, :] = a16
        dsl[rows, :] = sig * (1.0 + agg * (1.0 - sig))
        act_t[:, :, :, rows] = a16.T.reshape(2, 4, 64, A)

    def out_part(xd):
        return jnp.dot(
            act_t[:, pl.ds(xd, 1)].reshape(A, 2 * A), dout[...], preferred_element_type=F32
        )

    v = out_part(x2)
    so[0] = v[:64].astype(BF16)
    so[1] = v[64:].astype(BF16)
    sent.append(send(so.at[0], xo.at[0], s_xo.at[0], r_xo.at[0], right))
    sent.append(send(so.at[1], xo.at[1], s_xo.at[1], r_xo.at[1], left))
    v = out_part(xp)
    ko[0] = v[:64]
    so[2] = v[64:].astype(BF16)
    sent.append(send(so.at[2], xo.at[2], s_xo.at[2], r_xo.at[2], right))
    v = out_part(xn)
    so[3] = v[:64].astype(BF16)
    ko[1] = v[64:]
    sent.append(send(so.at[3], xo.at[3], s_xo.at[3], r_xo.at[3], left))
    v = out_part(x)
    ko[2] = v[:64]
    ko[3] = v[64:]

    for e in (0, 1):
        if e == 0:
            arrived(wob.at[0, xn], s_ox.at[0, 0], r_ox.at[0, 0], left)
            sent.append(send(wob.at[0, xn], wob.at[0, xn], s_ox.at[0, 2], r_ox.at[0, 2], right))
        else:
            arrived(wob.at[1, xp], s_ox.at[1, 1], r_ox.at[1, 1], right)
            sent.append(send(wob.at[1, xp], wob.at[1, xp], s_ox.at[1, 2], r_ox.at[1, 2], left))
    arrived(wob.at[0, xp], s_ox.at[0, 1], r_ox.at[0, 1], right)
    arrived(wob.at[1, xn], s_ox.at[1, 0], r_ox.at[1, 0], left)
    arrived(wob.at[0, x2], s_ox.at[0, 2], r_ox.at[0, 2], left)
    arrived(wob.at[1, x2], s_ox.at[1, 2], r_ox.at[1, 2], right)

    womat = wob[...].reshape(HC, C)
    for p in (0, 1):
        rows = slice(p * A, (p + 1) * A)
        dagg = contract(dout[rows, :], womat, 1, 1) * dsl[rows, :]
        for b in range(BASIS):
            rr[b * A : (b + 1) * A, :] = (dagg * radial[b : b + 1, mine_c]).astype(BF16)
        part = jnp.dot(mtc[p], rr[...], preferred_element_type=F32)
        if p == 0:
            spread[0:W, :] = part
            rim_s[0] = part[:H].astype(BF16)
        else:
            spread[A:W, :] = spread[A:W, :] + part[: W - A]
            spread[W:, :] = part[W - A :]
            rim_s[1] = part[W - H :].astype(BF16)

    def rim_dn():
        return pltpu.make_async_remote_copy(
            src_ref=rim_s.at[0], dst_ref=rim_hi, send_sem=s_misc.at[6], recv_sem=r_misc.at[6],
            device_id=chip(qp, c), device_id_type=MESH,
        )

    def rim_up():
        return pltpu.make_async_remote_copy(
            src_ref=rim_s.at[1], dst_ref=rim_lo, send_sem=s_misc.at[7], recv_sem=r_misc.at[7],
            device_id=chip(qn, c), device_id_type=MESH,
        )

    @pl.when(q > 0)
    def _():
        rim_dn().start()

    @pl.when(q < 15)
    def _():
        rim_up().start()

    arrived(xo.at[0], s_xo.at[0], r_xo.at[0], left)
    so[4] = (ko[0] + xo[0].astype(F32)).astype(BF16)
    sent.append(send(so.at[4], xo.at[4], s_xo.at[4], r_xo.at[4], right))
    arrived(xo.at[1], s_xo.at[1], r_xo.at[1], right)
    so[5] = (ko[1] + xo[1].astype(F32)).astype(BF16)
    sent.append(send(so.at[5], xo.at[5], s_xo.at[5], r_xo.at[5], left))

    @pl.when(q > 0)
    def _():
        arrived(rim_lo, s_misc.at[7], r_misc.at[7], chip(qp, c))

    @pl.when(q < 15)
    def _():
        arrived(rim_hi, s_misc.at[6], r_misc.at[6], chip(qn, c))

    dproj[0:H, :] = (spread[H : 2 * H, :] + rim_lo[...].astype(F32)).astype(BF16)
    dproj[H : 2 * A - H, :] = spread[2 * H : 2 * A, :].astype(BF16)
    dproj[2 * A - H :, :] = (spread[2 * A : 2 * A + H, :] + rim_hi[...].astype(F32)).astype(BF16)

    def msg_part(xd):
        v_ = jnp.dot(
            feats_t[:, pl.ds(xd, 1)].reshape(2 * A, 2 * A), dproj[...], preferred_element_type=F32
        )
        return v_[:A], v_[A:]

    lo, hi = msg_part(x2)
    sm[0] = lo.astype(BF16)
    sm[1] = hi.astype(BF16)
    sent.append(send(sm.at[0], xm.at[0], s_xm.at[0], r_xm.at[0], right))
    sent.append(send(sm.at[1], xm.at[1], s_xm.at[1], r_xm.at[1], left))
    lo, hi = msg_part(xp)
    km[0] = lo
    sm[2] = hi.astype(BF16)
    sent.append(send(sm.at[2], xm.at[2], s_xm.at[2], r_xm.at[2], right))
    lo, hi = msg_part(xn)
    sm[3] = lo.astype(BF16)
    km[1] = hi
    sent.append(send(sm.at[3], xm.at[3], s_xm.at[3], r_xm.at[3], left))
    lo, hi = msg_part(x)
    km[2] = lo
    km[3] = hi

    arrived(xo.at[3], s_xo.at[3], r_xo.at[3], right)
    arrived(xo.at[4], s_xo.at[4], r_xo.at[4], left)
    arrived(xo.at[2], s_xo.at[2], r_xo.at[2], left)
    arrived(xo.at[5], s_xo.at[5], r_xo.at[5], right)
    syo[0] = (ko[2] + xo[3].astype(F32) + xo[4].astype(F32)).astype(BF16).reshape(2, 32, C)
    syo[1] = (ko[3] + xo[2].astype(F32) + xo[5].astype(F32)).astype(BF16).reshape(2, 32, C)

    def yo_copy(e, c_):
        return pltpu.make_async_remote_copy(
            src_ref=syo.at[e, c_], dst_ref=yo.at[h],
            send_sem=s_yo.at[2 * e + c_], recv_sem=r_yo.at[h],
            device_id=dev(ylo, 2 * c + e, x, c_), device_id_type=MESH,
        )

    for e in (0, 1):
        for c_ in (0, 1):
            is_me = jnp.logical_and(2 * c + e == h, c == c_)

            @pl.when(jnp.logical_not(is_me))
            def _(e=e, c_=c_):
                yo_copy(e, c_).start()

            @pl.when(is_me)
            def _(e=e, c_=c_):
                cp = pltpu.make_async_copy(syo.at[e, c_], yo.at[h], loc.at[7])
                cp.start()
                cp.wait()

    womat = wob[...].reshape(HC, C)
    a_other = act[pl.ds(pl.multiple_of((1 - c) * A, A), A), :]
    part_s[...] = jnp.dot(a_other, womat, preferred_element_type=F32).astype(BF16)
    sent.append(send(part_s, part_r, s_misc.at[8], r_misc.at[8], partner))
    a_own = act[pl.ds(pl.multiple_of(c * A, A), A), :]
    node_own = jnp.dot(a_own, womat, preferred_element_type=F32) + feats[...].astype(F32)

    arrived(xm.at[0], s_xm.at[0], r_xm.at[0], left)
    sm[4] = (km[0] + xm[0].astype(F32)).astype(BF16)
    sent.append(send(sm.at[4], xm.at[4], s_xm.at[4], r_xm.at[4], right))
    arrived(xm.at[1], s_xm.at[1], r_xm.at[1], right)
    sm[5] = (km[1] + xm[1].astype(F32)).astype(BF16)
    sent.append(send(sm.at[5], xm.at[5], s_xm.at[5], r_xm.at[5], left))

    arrived(part_r, s_misc.at[8], r_misc.at[8], partner)
    node_o[...] = (node_own + part_r[...].astype(F32)).astype(BF16)

    for h_ in range(4):
        @pl.when(jnp.logical_or(h_ != h, c != half))
        def _(h_=h_):
            arrived(yo.at[h_], s_yo.at[0], r_yo.at[h_], dev(ylo, h_, x, half))

    total = yo[0].astype(F32) + yo[1].astype(F32) + yo[2].astype(F32) + yo[3].astype(F32)
    gout_o[0] = total.astype(BF16)
    gf[...] = total
    chosen = jnp.full((32, FRAG), frag[0], jnp.int32)

    def decoded():
        piece = jnp.zeros((32, FRAG), F32)
        for b in range(C // FRAG):
            piece = jnp.where(chosen == b, gf[:, b * FRAG : (b + 1) * FRAG], piece)
        scale = (jnp.max(jnp.abs(piece), axis=1, keepdims=True) + TINY).astype(BF16).astype(F32)
        code = (piece / scale).astype(BF16).astype(F32)
        return (scale * code).astype(BF16)

    def outer_send(m, buf, ss, rs):
        for d in range(1, 16):
            sent.append(send(tb.at[m], buf.at[r], ss.at[d], rs.at[d], ((r + d) % 16, f)))

    def outer_sum(m, buf, ss, rs):
        for d in range(1, 16):
            r_ = (r + 16 - d) % 16
            arrived(buf.at[r_], ss.at[d], rs.at[d], (r_, f))
        outer_o[m] = jnp.sum(buf[...].astype(F32), axis=0)

    term = decoded()
    tb[1] = term
    oo[r] = term
    outer_send(1, oo, s_oo, r_oo)

    arrived(xm.at[3], s_xm.at[3], r_xm.at[3], right)
    arrived(xm.at[4], s_xm.at[4], r_xm.at[4], left)
    arrived(xm.at[2], s_xm.at[2], r_xm.at[2], left)
    arrived(xm.at[5], s_xm.at[5], r_xm.at[5], right)
    lo = (km[2] + xm[3].astype(F32) + xm[4].astype(F32)).astype(BF16)
    hi = (km[3] + xm[2].astype(F32) + xm[5].astype(F32)).astype(BF16)
    sym[0:2] = lo.reshape(2, 2, 32, HC)
    sym[2:4] = hi.reshape(2, 2, 32, HC)
    keep = pltpu.make_async_copy(sym.at[h, c], ym.at[h, c], loc.at[8])
    keep.start()
    for d in range(7, 0, -1):
        hh, c_ = (h + d // 2) % 4, (c + d) % 2
        sent.append(
            send(sym.at[hh, c_], ym.at[h, c], s_ym.at[d], r_ym.at[d], dev(ylo, hh, x, c_))
        )
    outer_sum(1, oo, s_oo, r_oo)
    keep.wait()
    for d in range(1, 8):
        hh, c_ = (h + 4 - d // 2) % 4, (c + d) % 2
        arrived(ym.at[hh, c_], s_ym.at[d], r_ym.at[d], dev(ylo, hh, x, c_))
    for c_ in (0, 1):
        total = (
            ym[0, c_].astype(F32) + ym[1, c_].astype(F32)
            + ym[2, c_].astype(F32) + ym[3, c_].astype(F32)
        )
        gf[:, c_ * HC : (c_ + 1) * HC] = total
        gmsg_o[0, :, c_ * HC : (c_ + 1) * HC] = total.astype(BF16)
    term = decoded()
    tb[0] = term
    om[r] = term
    outer_send(0, om, s_om, r_om)
    outer_sum(0, om, s_om, r_om)

    for cp in sent:
        cp.wait_send()

    @pl.when(up_ok)
    def _():
        for c_ in (0, 1):
            up_copy(c_).wait_send()

    @pl.when(dn_ok)
    def _():
        for c_ in (0, 1):
            dn_copy(c_).wait_send()

    @pl.when(half != c)
    def _():
        wo_partner().wait_send()

    @pl.when(q > 0)
    def _():
        rim_dn().wait_send()

    @pl.when(q < 15)
    def _():
        rim_up().wait_send()

    for e in (0, 1):
        for c_ in (0, 1):
            @pl.when(jnp.logical_not(jnp.logical_and(2 * c + e == h, c == c_)))
            def _(e=e, c_=c_):
                yo_copy(e, c_).wait_send()


def shards(feats, src, dist, ids, wm, wo, radial, cot, frag):
    vm = pl.BlockSpec(memory_space=pltpu.VMEM)
    dma = lambda *n: pltpu.SemaphoreType.DMA(n)
    V = pltpu.VMEM
    return pl.pallas_call(
        body,
        out_shape=(
            jax.ShapeDtypeStruct((A, C), BF16),
            jax.ShapeDtypeStruct((1, 32, C), BF16),
            jax.ShapeDtypeStruct((1, 32, C), BF16),
            jax.ShapeDtypeStruct((2, 32, FRAG), F32),
        ),
        in_specs=[vm] * 8 + [pl.BlockSpec(memory_space=pltpu.SMEM)],
        out_specs=(vm,) * 4,
        scratch_shapes=[
            V((4, 4, 2, 32, HC), BF16),
            V((2, 4, 2, 32, C), BF16),
            V((4, 4, 2, 1, A), jnp.int32),
            V((EXT, C), BF16),
            V((2, A, C), BF16),
            V((2, NB, A), jnp.int32),
            V((2, NB, A), F32),
            V((A, C), BF16),
            V((H, HC), BF16),
            V((H, HC), BF16),
            V((6, 64, C), BF16),
            V((6, A, HC), BF16),
            V((4, 32, C), BF16),
            V((4, 2, 32, HC), BF16),
            V((16, 32, FRAG), BF16),
            V((16, 32, FRAG), BF16),
            V((BASIS, NB, A), F32),
            V((BASIS * W, A), F32),
            V((2, W, BASIS * A), BF16),
            V((2, A, BASIS * W), BF16),
            V((BASIS * W, HC), BF16),
            V((2 * A, HC), BF16),
            V((2 * A, HC), F32),
            V((2, 4, 64, 2 * A), BF16),
            V((4, 4, 64, 2 * A), BF16),
            V((2 * A, C), BF16),
            V((BASIS * A, HC), BF16),
            V((EXT, HC), F32),
            V((2 * A, HC), BF16),
            V((A, C), BF16),
            V((2, H, HC), BF16),
            V((6, 64, C), BF16),
            V((4, 64, C), F32),
            V((6, A, HC), BF16),
            V((4, A, HC), F32),
            V((2, 2, 32, C), BF16),
            V((4, 2, 32, HC), BF16),
            V((32, C), F32),
            V((2, 32, FRAG), BF16),
            dma(9),
            dma(7), dma(7), dma(7), dma(7), dma(4), dma(7),
            dma(4, 3), dma(4, 3), dma(4, 3), dma(4, 3), dma(2, 3), dma(2, 3),
            dma(9), dma(9), dma(6), dma(6), dma(6), dma(6),
            dma(4), dma(4), dma(8), dma(8), dma(16), dma(16), dma(16), dma(16),
        ],
        compiler_params=pltpu.CompilerParams(
            collective_id=0, has_side_effects=True, vmem_limit_bytes=56 << 20
        ),
        name="step",
    )(feats, src, dist, ids, wm, wo, radial, cot, frag)


def solution(mesh):
    placed = (
        P(("replica", "fsdp"), None),
        P(None, ("replica", "fsdp")),
        P(None, ("replica", "fsdp")),
        P("replica", "fsdp"),
        P("fsdp", None),
        P("fsdp", None),
        P(),
        P(("replica", "fsdp"), None),
        P(),
    )
    return jax.shard_map(
        shards,
        mesh=mesh,
        in_specs=placed,
        out_specs=(
            P(("replica", "fsdp"), None),
            P("replica", "fsdp", None),
            P("replica", "fsdp", None),
            P(None, "fsdp", None),
        ),
        check_vma=False,
    )
```

```python
import functools
import math

import jax
import jax.numpy as jnp
from jax import lax
from jax.experimental import pallas as pl
from jax.experimental.pallas import tpu as pltpu
from jax.sharding import PartitionSpec as P

MESH = pl.DeviceIdType.MESH
F32 = jnp.float32
BF16 = jnp.bfloat16
GRAPHS = 8
FRAG = 128
A = 128
C = 1024
HC = 512
H = 32
NB = 12
BASIS = 8
W = 2 * A - 64
EXT = 2 * A + 2 * H
TINY = 1e-6


def contract(a, b, da, db):
    return lax.dot_general(a, b, (((da,), (db,)), ((), ())), preferred_element_type=F32)


def body(
    feats, src, dist, ids, wm, wo, radial_h, cot, frag,
    node_o, gmsg_o, gout_o, outer_o,
    wmb, wob, wmv, wov, radial, idb, fx, cotb, srcb, distb, part_r,
    rim_lo, rim_hi, xo, xm, yo, ym, oo, om,
    bas, mtv, mtc, mc, ps, act, dsl, act_t, feats_t, dout, rr, spread, dproj,
    part_s, rim_s, so, ko, sm, km, syo, sym, gf, gm, tb,
    loc, s_wy, r_wy, s_iy, r_iy, s_oy, r_oy, s_wx, r_wx, s_wz, r_wz, s_ix, r_ix,
    s_ox, r_ox, s_oz, r_oz,
    s_misc, r_misc, s_xo, r_xo, s_xm, r_xm, s_yo, r_yo, s_ym, r_ym, s_oo, r_oo, s_om, r_om,
):
    r = lax.axis_index("replica")
    f = lax.axis_index("fsdp")
    ylo, z = r // 8, r % 8
    h, x, c = f // 8, (f // 2) % 4, f % 2
    q = f // 2
    s = 2 * ylo - 1
    xp, xn, x2 = (x + 1) % 4, (x + 3) % 4, (x + 2) % 4
    ha, hb, h2 = (h + s + 4) % 4, (h - s + 4) % 4, (h + 2) % 4
    half = h // 2
    par = z % 2

    def dev(ylo_, h_, x_, c_):
        return (ylo_ * 8 + z, h_ * 8 + x_ * 2 + c_)

    def chip(q_, c_):
        return (r, q_ * 2 + c_)

    partner = dev(ylo, h, x, 1 - c)
    right, left = dev(ylo, h, xp, c), dev(ylo, h, xn, c)
    qn, qp = (q + 1) % 16, (q + 15) % 16
    y_to = ((1 - ylo, ha), (ylo, ha), (1 - ylo, h2))
    y_in = (ha, hb, h2)
    y_from = ((1 - ylo, ha), (ylo, hb), (1 - ylo, h2))

    def send(a_, b_, ss, rs, to):
        cp = pltpu.make_async_remote_copy(
            src_ref=a_, dst_ref=b_, send_sem=ss, recv_sem=rs, device_id=to, device_id_type=MESH
        )
        cp.start()
        return cp

    def arrived(b_, ss, rs, frm):
        pltpu.make_async_remote_copy(
            src_ref=b_, dst_ref=b_, send_sem=ss, recv_sem=rs, device_id=frm, device_id_type=MESH
        ).wait_recv()

    bar = pltpu.get_barrier_semaphore()
    greet = [partner]
    for c_ in (0, 1):
        greet += [dev(ylo, h, x_, c_) for x_ in (xp, xn, x2)]
        greet += [
            dev(ylo, ha, x, c_), dev(ylo, hb, x, c_), dev(ylo, h2, x, c_),
            dev(1 - ylo, ha, x, c_), dev(1 - ylo, h2, x, c_), chip(qn, c_), chip(qp, c_),
        ]
    greet += [((r + d) % 16, f) for d in range(1, 16)]
    for g in greet:
        pl.semaphore_signal(bar, inc=1, device_id=g, device_id_type=MESH)

    f_rows = pl.ds(pl.multiple_of(H + A * c, H), A)
    f_other = pl.ds(pl.multiple_of(H + A * (1 - c), H), A)
    own = [
        pltpu.make_async_copy(a_, b_, loc.at[i])
        for i, (a_, b_) in enumerate(
            (
                (wm, wmv),
                (wm.at[:, pl.ds(pl.multiple_of(c * HC, HC), HC)], wmb.at[h, x, c]),
                (ids, idb.at[h, x, c]),
                (src, srcb.at[c]),
                (dist, distb.at[c]),
                (feats, fx.at[f_rows]),
                (wo, wov),
                (cot, cotb.at[c]),
                (radial_h, radial),
            )
        )
    ]
    for o in own:
        o.start()

    @pl.when(half == c)
    def _():
        cp = pltpu.make_async_copy(wo, wob.at[h % 2, x, c], loc.at[9])
        cp.start()
        cp.wait()

    @pl.when(q == 0)
    def _():
        fx[0:H, :] = jnp.zeros((H, C), BF16)
        rim_lo[...] = jnp.zeros((H, HC), BF16)

    @pl.when(q == 15)
    def _():
        fx[H + 2 * A :, :] = jnp.zeros((H, C), BF16)
        rim_hi[...] = jnp.zeros((H, HC), BF16)

    for o in own:
        o.wait()
    pl.semaphore_wait(bar, len(greet))

    sent = []
    other = pl.ds(pl.multiple_of((1 - c) * HC, HC), HC)
    mine_c = pl.ds(pl.multiple_of(c * HC, HC), HC)
    sent.append(send(wmv.at[:, other], wmb.at[h, x, c], s_wy.at[6], r_wy.at[6], partner))

    def wm_y(j, c_):
        yl, hh = y_to[j]
        return pltpu.make_async_remote_copy(
            src_ref=wmv.at[:, pl.ds(c_ * HC, HC)], dst_ref=wmb.at[h, x, c],
            send_sem=s_wy.at[2 * j + c_], recv_sem=r_wy.at[2 * j + c],
            device_id=dev(yl, hh, x, c_), device_id_type=MESH,
        )

    def wo_y(j):
        yl, hh = y_to[j]
        return pltpu.make_async_remote_copy(
            src_ref=wov, dst_ref=wob.at[h % 2, x, c],
            send_sem=s_oy.at[j], recv_sem=r_oy.at[2 * j + c],
            device_id=dev(yl, hh, x, half), device_id_type=MESH,
        )

    y_of = ((2,), (0, 1))
    for parity in (0, 1):
        @pl.when(par == parity)
        def _(parity=parity):
            for j in y_of[parity]:
                for c_ in (0, 1):
                    wm_y(j, c_).start()

    @pl.when(h % 2 == par)
    def _():
        for j in (2, 1, 0):
            wo_y(j).start()

    sent.append(send(srcb.at[c], srcb.at[c], s_misc.at[0], r_misc.at[0], partner))
    sent.append(send(distb.at[c], distb.at[c], s_misc.at[1], r_misc.at[1], partner))
    my_ids = idb.at[h, x, c]
    sent.append(send(my_ids, my_ids, s_iy.at[6], r_iy.at[6], partner))
    for j, hh in enumerate((hb, ha, h2)):
        for c_ in (0, 1):
            sent.append(
                send(
                    my_ids, my_ids, s_iy.at[2 * j + c_], r_iy.at[2 * j + c], dev(ylo, hh, x, c_)
                )
            )

    def wm_in(k):
        if k == 0:
            arrived(wmb.at[h, x, 1 - c], s_wy.at[6], r_wy.at[6], partner)
        else:
            for c_ in (0, 1):
                i = 2 * (k - 1) + c_
                arrived(
                    wmb.at[y_in[k - 1], x, c_], s_wy.at[i], r_wy.at[i], dev(*y_from[k - 1], x, c_)
                )

    taken = ((h + par * s + 4) % 4, (h + 2 * (1 - par) - par * s + 4) % 4)
    rest = ((h + (1 - par) * s + 4) % 4, (h + 2 * par - (1 - par) * s + 4) % 4)
    z_to = ((ylo * 8 + (z + 1) % 8, f), (ylo * 8 + (z + 7) % 8, f))
    z_in = (z_to[1], z_to[0])

    far = dev(ylo, h, x2, c)

    def wm_x(n, i):
        ref = wmb.at[taken[n], x]
        return pltpu.make_async_remote_copy(
            src_ref=ref, dst_ref=ref, send_sem=s_wx.at[n, i], recv_sem=r_wx.at[n, i],
            device_id=(right, left, far)[i], device_id_type=MESH,
        )

    def wm_z(n, i, u):
        ref = wmb.at[taken[n], (xn, xp, x2, x)[i], u]
        return pltpu.make_async_remote_copy(
            src_ref=ref, dst_ref=ref, send_sem=s_wz.at[n, i, u], recv_sem=r_wz.at[n, i, u],
            device_id=z_to[u], device_id_type=MESH,
        )

    def wm_x_start(n, parity):
        @pl.when(par == parity)
        def _():
            if n or parity:
                wm_in(3 if parity == 0 else 1 + n)
            for i in range(3):
                wm_x(n, i).start()
            if n or parity:
                for u in (0, 1):
                    wm_z(n, 3, u).start()

    def wm_x_in(n, i):
        ref = wmb.at[taken[n], (xn, xp, x2)[i]]
        arrived(ref, s_wx.at[n, i], r_wx.at[n, i], (left, right, far)[i])
        for u in (0, 1):
            wm_z(n, i, u).start()

    norm = 1.0 / math.sqrt(NB)
    PARTS = 2

    def build(p, part):
        if part == 0:
            d = distb[p]
            env = 0.5 * (jnp.cos(d * (math.pi / 5.0)) + 1.0) * norm
            for b in range(BASIS):
                bas[b] = jnp.exp(-2.0 * (d - 5.0 * b / (BASIS - 1)) ** 2) * env
        base = 2 * A * q - H + A * p

        def tile(t, carry):
            row = pl.multiple_of(t * 16, 16)
            at = row + base + lax.broadcasted_iota(jnp.int32, (16, A), 0)
            accs = [jnp.zeros((16, A), F32) for _ in range(BASIS)]
            for k in range(NB):
                hit = srcb[p, k : k + 1, :] == at
                for b in range(BASIS):
                    accs[b] = accs[b] + jnp.where(hit, bas[b, k : k + 1, :], 0.0)
            for b in range(BASIS):
                mtv[pl.ds(pl.multiple_of(b * W + row, 16), 16), :] = accs[b]
                mtc[p, pl.ds(row, 16), b * A : (b + 1) * A] = accs[b].astype(BF16)
            return carry

        step = W // 16 // PARTS
        lax.fori_loop(part * step, (part + 1) * step, tile, 0)
        if part == PARTS - 1:
            for t in range(BASIS * W // A):
                mc[p, :, t * A : (t + 1) * A] = mtv[t * A : (t + 1) * A, :].T.astype(BF16)

    wm_in(0)
    wm_x_start(0, 0)

    def wo_partner():
        return pltpu.make_async_remote_copy(
            src_ref=wov, dst_ref=wob.at[h % 2, x, c], send_sem=s_oy.at[3], recv_sem=r_oy.at[6],
            device_id=partner, device_id_type=MESH,
        )

    @pl.when(half != c)
    def _():
        wo_partner().start()

    up_ok = jnp.logical_and(c == 1, q < 15)
    dn_ok = jnp.logical_and(c == 0, q > 0)

    def up_copy(c_):
        return pltpu.make_async_remote_copy(
            src_ref=fx.at[pl.ds(2 * A, H)], dst_ref=fx.at[pl.ds(0, H)],
            send_sem=s_misc.at[4 + c_], recv_sem=r_misc.at[4],
            device_id=chip(qn, c_), device_id_type=MESH,
        )

    def dn_copy(c_):
        return pltpu.make_async_remote_copy(
            src_ref=fx.at[pl.ds(H, H)], dst_ref=fx.at[pl.ds(H + 2 * A, H)],
            send_sem=s_misc.at[4 + c_], recv_sem=r_misc.at[5],
            device_id=chip(qp, c_), device_id_type=MESH,
        )

    @pl.when(up_ok)
    def _():
        for c_ in (0, 1):
            up_copy(c_).start()

    @pl.when(dn_ok)
    def _():
        for c_ in (0, 1):
            dn_copy(c_).start()

    sent.append(send(fx.at[f_rows], fx.at[f_rows], s_misc.at[2], r_misc.at[2], partner))
    sent.append(send(cotb.at[c], cotb.at[c], s_misc.at[3], r_misc.at[3], partner))

    def wo_in():
        @pl.when(h == 2 * c + par)
        def _():
            arrived(wob.at[par, x, 1 - c], s_oy.at[3], r_oy.at[6], partner)

        for j in range(3):
            @pl.when(y_in[j] == 2 * c + par)
            def _(j=j):
                for c_ in (0, 1):
                    arrived(
                        wob.at[par, x, c_], s_oy.at[0], r_oy.at[2 * j + c_],
                        dev(*y_from[j], x, c_),
                    )

        for i, to in enumerate((right, left, far)):
            ref = wob.at[par, x]
            sent.append(send(ref, ref, s_ox.at[i], r_ox.at[i], to))

    def wo_own_z(u):
        ref = wob.at[par, x, u]
        return pltpu.make_async_remote_copy(
            src_ref=ref, dst_ref=ref, send_sem=s_oz.at[3, u], recv_sem=r_oz.at[3, u],
            device_id=z_to[u], device_id_type=MESH,
        )

    def wo_z():
        @pl.when(h != 2 * c + par)
        def _():
            for u in (0, 1):
                wo_own_z(u).start()

    def wo_x_in(i):
        col = (xn, xp, x2)[i]
        arrived(wob.at[par, col], s_ox.at[i], r_ox.at[i], (left, right, far)[i])
        for u in (0, 1):
            ref = wob.at[par, col, u]
            sent.append(send(ref, ref, s_oz.at[i, u], r_oz.at[i, u], z_to[u]))

    arrived(srcb.at[1 - c], s_misc.at[0], r_misc.at[0], partner)
    arrived(distb.at[1 - c], s_misc.at[1], r_misc.at[1], partner)
    build(0, 0)
    wm_x_start(0, 1)
    wm_x_start(1, 0)
    wm_x_start(1, 1)
    arrived(idb.at[h, x, 1 - c], s_iy.at[6], r_iy.at[6], partner)
    for k, yb in enumerate(y_in):
        for c_ in (0, 1):
            i = 2 * k + c_
            arrived(idb.at[yb, x, c_], s_iy.at[i], r_iy.at[i], dev(ylo, yb, x, c_))
    for i, x_ in enumerate((xp, xn, x2)):
        ref = idb.at[:, x]
        sent.append(send(ref, ref, s_ix.at[i], r_ix.at[i], dev(ylo, h, x_, c)))
    build(0, 1)
    wo_in()
    wm_x_in(0, 0)
    wm_x_in(0, 1)
    build(1, 0)
    wm_x_in(0, 2)
    wm_x_in(1, 1)
    wm_x_in(1, 0)
    wm_x_in(1, 2)
    build(1, 1)
    arrived(fx.at[f_other], s_misc.at[2], r_misc.at[2], partner)
    for p in (0, 1):
        feats_t[:, :, :, p * A : (p + 1) * A] = (
            fx[H + p * A : H + (p + 1) * A, :].T.reshape(4, 4, 64, A)
        )
    arrived(cotb.at[1 - c], s_misc.at[3], r_misc.at[3], partner)

    @pl.when(q > 0)
    def _():
        arrived(fx.at[pl.ds(0, H)], s_misc.at[4], r_misc.at[4], chip(qp, 1))

    @pl.when(q < 15)
    def _():
        arrived(fx.at[pl.ds(H + 2 * A, H)], s_misc.at[4], r_misc.at[5], chip(qn, 0))

    wo_z()
    wo_x_in(0)
    wo_x_in(1)
    for i, x_ in enumerate((xn, xp, x2)):
        arrived(idb.at[:, x_], s_ix.at[i], r_ix.at[i], dev(ylo, h, x_, c))
    all_ids = idb[...].reshape(32, A)
    for p in (0, 1):
        mine = idb[h, x, p]
        wrow = jnp.zeros((1, A), F32)
        for g in range(GRAPHS):
            count = jnp.sum((all_ids == g).astype(F32), axis=0, keepdims=True)
            count = jnp.sum(count, axis=1, keepdims=True)
            wrow = wrow + jnp.where(mine == g, lax.rsqrt(jnp.broadcast_to(count, (1, A))), 0.0)
        wcol = jnp.broadcast_to(wrow, (A, A)).T
        for t in range(C // A):
            cols = slice(t * A, (t + 1) * A)
            dout[p * A : (p + 1) * A, cols] = (cotb[p, :, cols].astype(F32) * wcol).astype(BF16)

    for n in (0, 1):
        for i, col in enumerate((xn, xp, x2)):
            for u in (0, 1):
                arrived(wmb.at[rest[n], col, u], s_wz.at[n, i, u], r_wz.at[n, i, u], z_in[u])
        if n:
            for u in (0, 1):
                arrived(wmb.at[rest[n], x, u], s_wz.at[n, 3, u], r_wz.at[n, 3, u], z_in[u])
        else:
            @pl.when(par == 0)
            def _():
                for u in (0, 1):
                    arrived(wmb.at[rest[0], x, u], s_wz.at[0, 3, u], r_wz.at[0, 3, u], z_in[u])

    wmat = wmb[...].reshape(C, HC)
    proj = jnp.dot(fx[...], wmat, preferred_element_type=F32).astype(BF16)
    spread[...] = proj.astype(F32)
    for p in (0, 1):
        for b in range(BASIS):
            ps[b * W : (b + 1) * W, :] = (
                spread[p * A : p * A + W, :] * radial[b : b + 1, mine_c]
            ).astype(BF16)
        agg = jnp.dot(mc[p], ps[...], preferred_element_type=F32)
        sig = 1.0 / (1.0 + jnp.exp(-agg))
        a16 = (agg * sig).astype(BF16)
        rows = slice(p * A, (p + 1) * A)
        act[rows, :] = a16
        dsl[rows, :] = sig * (1.0 + agg * (1.0 - sig))
        act_t[:, :, :, rows] = a16.T.reshape(2, 4, 64, A)

    wo_x_in(2)
    def out_part(xd):
        return jnp.dot(
            act_t[:, pl.ds(xd, 1)].reshape(A, 2 * A), dout[...], preferred_element_type=F32
        )

    v = out_part(x2)
    so[0] = v[:64].astype(BF16)
    so[1] = v[64:].astype(BF16)
    sent.append(send(so.at[0], xo.at[0], s_xo.at[0], r_xo.at[0], right))
    sent.append(send(so.at[1], xo.at[1], s_xo.at[1], r_xo.at[1], left))
    v = out_part(xp)
    ko[0] = v[:64]
    so[2] = v[64:].astype(BF16)
    sent.append(send(so.at[2], xo.at[2], s_xo.at[2], r_xo.at[2], right))
    v = out_part(xn)
    so[3] = v[:64].astype(BF16)
    ko[1] = v[64:]
    sent.append(send(so.at[3], xo.at[3], s_xo.at[3], r_xo.at[3], left))
    v = out_part(x)
    ko[2] = v[:64]
    ko[3] = v[64:]

    arrived(xo.at[0], s_xo.at[0], r_xo.at[0], left)
    so[4] = (ko[0] + xo[0].astype(F32)).astype(BF16)
    sent.append(send(so.at[4], xo.at[4], s_xo.at[4], r_xo.at[4], right))
    arrived(xo.at[1], s_xo.at[1], r_xo.at[1], right)
    so[5] = (ko[1] + xo[1].astype(F32)).astype(BF16)
    sent.append(send(so.at[5], xo.at[5], s_xo.at[5], r_xo.at[5], left))

    for i, x_ in enumerate((xn, xp, x2)):
        for u in (0, 1):
            arrived(wob.at[1 - par, x_, u], s_oz.at[i, u], r_oz.at[i, u], z_in[u])

    @pl.when(h != 2 * c + 1 - par)
    def _():
        for u in (0, 1):
            arrived(wob.at[1 - par, x, u], s_oz.at[3, u], r_oz.at[3, u], z_in[u])

    @pl.when(h == 2 * c + 1 - par)
    def _():
        arrived(wob.at[1 - par, x, 1 - c], s_oy.at[3], r_oy.at[6], partner)

    womat = wob[...].reshape(HC, C)
    for p in (0, 1):
        rows = slice(p * A, (p + 1) * A)
        dagg = contract(dout[rows, :], womat, 1, 1) * dsl[rows, :]
        for b in range(BASIS):
            rr[b * A : (b + 1) * A, :] = (dagg * radial[b : b + 1, mine_c]).astype(BF16)
        part = jnp.dot(mtc[p], rr[...], preferred_element_type=F32)
        if p == 0:
            spread[0:W, :] = part
            rim_s[0] = part[:H].astype(BF16)
        else:
            spread[A:W, :] = spread[A:W, :] + part[: W - A]
            spread[W:, :] = part[W - A :]
            rim_s[1] = part[W - H :].astype(BF16)

    def rim_dn():
        return pltpu.make_async_remote_copy(
            src_ref=rim_s.at[0], dst_ref=rim_hi, send_sem=s_misc.at[6], recv_sem=r_misc.at[6],
            device_id=chip(qp, c), device_id_type=MESH,
        )

    def rim_up():
        return pltpu.make_async_remote_copy(
            src_ref=rim_s.at[1], dst_ref=rim_lo, send_sem=s_misc.at[7], recv_sem=r_misc.at[7],
            device_id=chip(qn, c), device_id_type=MESH,
        )

    @pl.when(q > 0)
    def _():
        rim_dn().start()

    @pl.when(q < 15)
    def _():
        rim_up().start()

    @pl.when(q > 0)
    def _():
        arrived(rim_lo, s_misc.at[7], r_misc.at[7], chip(qp, c))

    @pl.when(q < 15)
    def _():
        arrived(rim_hi, s_misc.at[6], r_misc.at[6], chip(qn, c))

    spread[H : 2 * H, :] = spread[H : 2 * H, :] + rim_lo[...].astype(F32)
    spread[2 * A : 2 * A + H, :] = spread[2 * A : 2 * A + H, :] + rim_hi[...].astype(F32)

    def turned(rows, back, blocks):
        which = jnp.full((rows, FRAG), frag[0], jnp.int32)
        res = []
        for k in range(4):
            v_ = blocks(k)
            for o in range(1, 4):
                hit = jnp.logical_or(which == o, which == o + 4)
                v_ = jnp.where(hit, blocks((k - o if back else k + o) % 4), v_)
            res.append(v_)
        return res

    for k, v in enumerate(
        turned(2 * A, False, lambda k: spread[H : H + 2 * A, k * FRAG : (k + 1) * FRAG])
    ):
        dproj[:, k * FRAG : (k + 1) * FRAG] = v.astype(BF16)

    def msg_part(xd, store_lo, store_hi):
        v_ = jnp.dot(
            feats_t[:, pl.ds(xd, 1)].reshape(2 * A, 2 * A), dproj[...], preferred_element_type=F32
        )
        for k in range(4):
            store_lo(k, v_[:A, k * FRAG : (k + 1) * FRAG])
            store_hi(k, v_[A:, k * FRAG : (k + 1) * FRAG])

    def staged(i):
        def f_(k, v_):
            sm[k, i] = v_.astype(BF16)
        return f_

    def kept(i):
        def f_(k, v_):
            km[k, i] = v_
        return f_

    msg_part(x2, staged(0), staged(1))
    msg_part(xp, kept(0), staged(2))
    msg_part(xn, staged(3), kept(1))
    msg_part(x, kept(2), kept(3))

    def msg_leg(k, i):
        to = (right, left, right, left, right, left)[i]
        sent.append(send(sm.at[k, i], xm.at[k, i], s_xm.at[k, i], r_xm.at[k, i], to))

    def msg_in(k, i):
        frm = (left, right, left, right, left, right)[i]
        arrived(xm.at[k, i], s_xm.at[k, i], r_xm.at[k, i], frm)

    def msg_first(k):
        for i in range(4):
            msg_leg(k, i)

    def msg_relay(k):
        for i in (0, 1):
            msg_in(k, i)
            sm[k, 4 + i] = (km[k, i] + xm[k, i].astype(F32)).astype(BF16)
            msg_leg(k, 4 + i)

    def msg_y(k):
        for i in (2, 3, 4, 5):
            msg_in(k, i)
        lo = (km[k, 2] + xm[k, 3].astype(F32) + xm[k, 4].astype(F32)).astype(BF16)
        hi = (km[k, 3] + xm[k, 2].astype(F32) + xm[k, 5].astype(F32)).astype(BF16)
        sym[k, 0:2] = lo.reshape(2, 2, 32, FRAG)
        sym[k, 2:4] = hi.reshape(2, 2, 32, FRAG)
        for d in range(7, 0, -1):
            hh, c_ = (h + d // 2) % 4, (c + d) % 2
            sent.append(
                send(
                    sym.at[k, hh, c_], ym.at[k, h, c], s_ym.at[k, d], r_ym.at[k, d],
                    dev(ylo, hh, x, c_),
                )
            )
        ym[k, h, c] = sym[k, h, c]

    def msg_sum(k):
        for d in range(1, 8):
            hh, c_ = (h + 4 - d // 2) % 4, (c + d) % 2
            arrived(ym.at[k, hh, c_], s_ym.at[k, d], r_ym.at[k, d], dev(ylo, hh, x, c_))
        for c_ in (0, 1):
            gm[c_, k] = (
                ym[k, 0, c_].astype(F32) + ym[k, 1, c_].astype(F32)
                + ym[k, 2, c_].astype(F32) + ym[k, 3, c_].astype(F32)
            )

    msg_first(0)
    msg_first(1)

    arrived(xo.at[3], s_xo.at[3], r_xo.at[3], right)
    arrived(xo.at[4], s_xo.at[4], r_xo.at[4], left)
    arrived(xo.at[2], s_xo.at[2], r_xo.at[2], left)
    arrived(xo.at[5], s_xo.at[5], r_xo.at[5], right)
    syo[0] = (ko[2] + xo[3].astype(F32) + xo[4].astype(F32)).astype(BF16).reshape(2, 32, C)
    syo[1] = (ko[3] + xo[2].astype(F32) + xo[5].astype(F32)).astype(BF16).reshape(2, 32, C)

    def yo_copy(e, c_):
        return pltpu.make_async_remote_copy(
            src_ref=syo.at[e, c_], dst_ref=yo.at[h],
            send_sem=s_yo.at[2 * e + c_], recv_sem=r_yo.at[h],
            device_id=dev(ylo, 2 * c + e, x, c_), device_id_type=MESH,
        )

    for e in (0, 1):
        for c_ in (0, 1):
            is_me = jnp.logical_and(2 * c + e == h, c == c_)

            @pl.when(jnp.logical_not(is_me))
            def _(e=e, c_=c_):
                yo_copy(e, c_).start()

            @pl.when(is_me)
            def _(e=e, c_=c_):
                cp = pltpu.make_async_copy(syo.at[e, c_], yo.at[h], loc.at[7])
                cp.start()
                cp.wait()

    womat = wob[...].reshape(HC, C)
    a_other = act[pl.ds(pl.multiple_of((1 - c) * A, A), A), :]
    part_s[...] = jnp.dot(a_other, womat, preferred_element_type=F32).astype(BF16)
    sent.append(send(part_s, part_r, s_misc.at[8], r_misc.at[8], partner))
    a_own = act[pl.ds(pl.multiple_of(c * A, A), A), :]
    node_own = jnp.dot(a_own, womat, preferred_element_type=F32) + fx[f_rows, :].astype(F32)

    msg_relay(0)
    msg_first(2)
    msg_relay(1)
    msg_first(3)
    msg_y(0)
    msg_relay(2)
    msg_y(1)
    msg_relay(3)
    for h_ in range(4):
        @pl.when(jnp.logical_or(h_ != h, c != half))
        def _(h_=h_):
            arrived(yo.at[h_], s_yo.at[0], r_yo.at[h_], dev(ylo, h_, x, half))

    total = yo[0].astype(F32) + yo[1].astype(F32) + yo[2].astype(F32) + yo[3].astype(F32)
    gout_o[0] = total.astype(BF16)
    gf[...] = total
    chosen = jnp.full((32, FRAG), frag[0], jnp.int32)

    def decoded(piece):
        scale = (jnp.max(jnp.abs(piece), axis=1, keepdims=True) + TINY).astype(BF16).astype(F32)
        code = (piece / scale).astype(BF16).astype(F32)
        return (scale * code).astype(BF16)

    def outer_send(m, buf, ss, rs):
        for d in range(1, 16):
            sent.append(send(tb.at[m], buf.at[r], ss.at[d], rs.at[d], ((r + d) % 16, f)))

    def outer_sum(m, buf, ss, rs):
        for d in range(1, 16):
            r_ = (r + 16 - d) % 16
            arrived(buf.at[r_], ss.at[d], rs.at[d], (r_, f))
        outer_o[m] = jnp.sum(buf[...].astype(F32), axis=0)

    piece = jnp.zeros((32, FRAG), F32)
    for b in range(C // FRAG):
        piece = jnp.where(chosen == b, gf[:, b * FRAG : (b + 1) * FRAG], piece)
    term = decoded(piece)
    tb[1] = term
    oo[r] = term
    outer_send(1, oo, s_oo, r_oo)

    msg_y(2)
    msg_y(3)
    msg_sum(0)
    term = decoded(jnp.where(chosen < 4, gm[0, 0], gm[1, 0]))
    tb[0] = term
    om[r] = term
    outer_send(0, om, s_om, r_om)
    arrived(part_r, s_misc.at[8], r_misc.at[8], partner)
    node_o[...] = (node_own + part_r[...].astype(F32)).astype(BF16)
    outer_sum(1, oo, s_oo, r_oo)
    for k in (1, 2, 3):
        msg_sum(k)
    for c_ in (0, 1):
        for k, v in enumerate(turned(32, True, lambda k: gm[c_, k])):
            gmsg_o[0, :, c_ * HC + k * FRAG : c_ * HC + (k + 1) * FRAG] = v.astype(BF16)
    outer_sum(0, om, s_om, r_om)

    for cp in sent:
        cp.wait_send()

    @pl.when(up_ok)
    def _():
        for c_ in (0, 1):
            up_copy(c_).wait_send()

    @pl.when(dn_ok)
    def _():
        for c_ in (0, 1):
            dn_copy(c_).wait_send()

    @pl.when(half != c)
    def _():
        wo_partner().wait_send()

    for n in (0, 1):
        for i in range(3):
            wm_x(n, i).wait_send()
        for i in range(3):
            for u in (0, 1):
                wm_z(n, i, u).wait_send()
    for u in (0, 1):
        wm_z(1, 3, u).wait_send()

    for parity in (0, 1):
        @pl.when(par == parity)
        def _(parity=parity):
            for j in y_of[parity]:
                for c_ in (0, 1):
                    wm_y(j, c_).wait_send()
            if parity:
                for u in (0, 1):
                    wm_z(0, 3, u).wait_send()

    @pl.when(h % 2 == par)
    def _():
        for j in range(3):
            wo_y(j).wait_send()

    @pl.when(h != 2 * c + par)
    def _():
        for u in (0, 1):
            wo_own_z(u).wait_send()
    @pl.when(q > 0)
    def _():
        rim_dn().wait_send()

    @pl.when(q < 15)
    def _():
        rim_up().wait_send()

    for e in (0, 1):
        for c_ in (0, 1):
            @pl.when(jnp.logical_not(jnp.logical_and(2 * c + e == h, c == c_)))
            def _(e=e, c_=c_):
                yo_copy(e, c_).wait_send()


def shards(feats, src, dist, ids, wm, wo, radial, cot, frag):
    vm = pl.BlockSpec(memory_space=pltpu.VMEM)
    dma = lambda *n: pltpu.SemaphoreType.DMA(n)
    V = pltpu.VMEM
    return pl.pallas_call(
        body,
        out_shape=(
            jax.ShapeDtypeStruct((A, C), BF16),
            jax.ShapeDtypeStruct((1, 32, C), BF16),
            jax.ShapeDtypeStruct((1, 32, C), BF16),
            jax.ShapeDtypeStruct((2, 32, FRAG), F32),
        ),
        in_specs=[pl.BlockSpec(memory_space=pl.ANY)] * 8 + [pl.BlockSpec(memory_space=pltpu.SMEM)],
        out_specs=(vm,) * 4,
        scratch_shapes=[
            V((4, 4, 2, 32, HC), BF16),
            V((2, 4, 2, 32, C), BF16),
            V((32, C), BF16),
            V((32, C), BF16),
            V((BASIS, C), F32),
            V((4, 4, 2, 1, A), jnp.int32),
            V((EXT, C), BF16),
            V((2, A, C), BF16),
            V((2, NB, A), jnp.int32),
            V((2, NB, A), F32),
            V((A, C), BF16),
            V((H, HC), BF16),
            V((H, HC), BF16),
            V((6, 64, C), BF16),
            V((4, 6, A, FRAG), BF16),
            V((4, 32, C), BF16),
            V((4, 4, 2, 32, FRAG), BF16),
            V((16, 32, FRAG), BF16),
            V((16, 32, FRAG), BF16),
            V((BASIS, NB, A), F32),
            V((BASIS * W, A), F32),
            V((2, W, BASIS * A), BF16),
            V((2, A, BASIS * W), BF16),
            V((BASIS * W, HC), BF16),
            V((2 * A, HC), BF16),
            V((2 * A, HC), F32),
            V((2, 4, 64, 2 * A), BF16),
            V((4, 4, 64, 2 * A), BF16),
            V((2 * A, C), BF16),
            V((BASIS * A, HC), BF16),
            V((EXT, HC), F32),
            V((2 * A, HC), BF16),
            V((A, C), BF16),
            V((2, H, HC), BF16),
            V((6, 64, C), BF16),
            V((4, 64, C), F32),
            V((4, 6, A, FRAG), BF16),
            V((4, 4, A, FRAG), F32),
            V((2, 2, 32, C), BF16),
            V((4, 4, 2, 32, FRAG), BF16),
            V((32, C), F32),
            V((2, 4, 32, FRAG), F32),
            V((2, 32, FRAG), BF16),
            dma(10),
            dma(7), dma(7), dma(7), dma(7), dma(4), dma(7),
            dma(2, 3), dma(2, 3), dma(2, 4, 2), dma(2, 4, 2), dma(3), dma(3),
            dma(4), dma(4), dma(4, 2), dma(4, 2),
            dma(9), dma(9), dma(6), dma(6), dma(4, 6), dma(4, 6),
            dma(4), dma(4), dma(4, 8), dma(4, 8), dma(16), dma(16), dma(16), dma(16),
        ],
        compiler_params=pltpu.CompilerParams(
            collective_id=0, has_side_effects=True, vmem_limit_bytes=56 << 20
        ),
        name="step",
    )(feats, src, dist, ids, wm, wo, radial, cot, frag)


def solution(mesh):
    placed = (
        P(("replica", "fsdp"), None),
        P(None, ("replica", "fsdp")),
        P(None, ("replica", "fsdp")),
        P("replica", "fsdp"),
        P("fsdp", None),
        P("fsdp", None),
        P(),
        P(("replica", "fsdp"), None),
        P(),
    )
    return jax.shard_map(
        shards,
        mesh=mesh,
        in_specs=placed,
        out_specs=(
            P(("replica", "fsdp"), None),
            P("replica", "fsdp", None),
            P("replica", "fsdp", None),
            P(None, "fsdp", None),
        ),
        check_vma=False,
    )
```

```python
import functools
import math

import jax
import jax.numpy as jnp
from jax import lax
from jax.experimental import pallas as pl
from jax.experimental.pallas import tpu as pltpu
from jax.sharding import PartitionSpec as P

MESH = pl.DeviceIdType.MESH
F32 = jnp.float32
BF16 = jnp.bfloat16
GRAPHS = 8
FRAG = 128
A = 128
C = 1024
HC = 512
H = 32
NB = 12
BASIS = 8
W = 2 * A - 64
EXT = 2 * A + 2 * H
TINY = 1e-6


def contract(a, b, da, db):
    return lax.dot_general(a, b, (((da,), (db,)), ((), ())), preferred_element_type=F32)


def body(
    feats, src, dist, ids, wm, wo, radial_h, cot, frag,
    node_h, gmsg_h, gout_h, outer_h,
    wmb, wob, wmv, wov, radial, idb, fx, cotb, srcb, distb, part_r,
    rim_lo, rim_hi, xo, xm, yo, ym, oo, om,
    bas, mtv, mtc, mc, ps, act, dsl, act_t, feats_t, dout, rr, spread, dproj,
    part_s, rim_s, so, ko, sm, km, syo, sym, gf, gm, tb, node_o, gmsg_o, gout_o, outer_o,
    loc, s_wy, r_wy, s_iy, r_iy, s_oy, r_oy, s_wx, r_wx, s_wz, r_wz, s_ix, r_ix,
    s_ox, r_ox, s_oz, r_oz,
    s_misc, r_misc, s_xo, r_xo, s_xm, r_xm, s_yo, r_yo, s_ym, r_ym, s_oo, r_oo, s_om, r_om,
):
    r = lax.axis_index("replica")
    f = lax.axis_index("fsdp")
    ylo, z = r // 8, r % 8
    h, x, c = f // 8, (f // 2) % 4, f % 2
    q = f // 2
    s = 2 * ylo - 1
    xp, xn, x2 = (x + 1) % 4, (x + 3) % 4, (x + 2) % 4
    ha, hb, h2 = (h + s + 4) % 4, (h - s + 4) % 4, (h + 2) % 4
    half = h // 2
    par = z % 2

    def dev(ylo_, h_, x_, c_):
        return (ylo_ * 8 + z, h_ * 8 + x_ * 2 + c_)

    def chip(q_, c_):
        return (r, q_ * 2 + c_)

    partner = dev(ylo, h, x, 1 - c)
    right, left = dev(ylo, h, xp, c), dev(ylo, h, xn, c)
    qn, qp = (q + 1) % 16, (q + 15) % 16
    y_to = ((1 - ylo, ha), (ylo, ha), (1 - ylo, h2))
    y_in = (ha, hb, h2)
    y_from = ((1 - ylo, ha), (ylo, hb), (1 - ylo, h2))

    def send(a_, b_, ss, rs, to):
        cp = pltpu.make_async_remote_copy(
            src_ref=a_, dst_ref=b_, send_sem=ss, recv_sem=rs, device_id=to, device_id_type=MESH
        )
        cp.start()
        return cp

    def arrived(b_, ss, rs, frm):
        pltpu.make_async_remote_copy(
            src_ref=b_, dst_ref=b_, send_sem=ss, recv_sem=rs, device_id=frm, device_id_type=MESH
        ).wait_recv()

    def put(i, a_, b_):
        cp = pltpu.make_async_copy(a_, b_, loc.at[10 + i])
        cp.start()
        puts.append(cp)

    puts = []
    def both(ref, ss, rs):
        return pltpu.make_async_remote_copy(
            src_ref=ref, dst_ref=ref, send_sem=ss, recv_sem=rs, device_id=partner,
            device_id_type=MESH,
        )

    bar = pltpu.get_barrier_semaphore()
    greet = [partner]
    for c_ in (0, 1):
        greet += [dev(ylo, h, x_, c_) for x_ in (xp, xn, x2)]
        greet += [
            dev(ylo, ha, x, c_), dev(ylo, hb, x, c_), dev(ylo, h2, x, c_),
            dev(1 - ylo, ha, x, c_), dev(1 - ylo, h2, x, c_), chip(qn, c_), chip(qp, c_),
        ]
    greet += [((r + d) % 16, f) for d in range(1, 16)]
    for g in greet:
        pl.semaphore_signal(bar, inc=1, device_id=g, device_id_type=MESH)

    f_rows = pl.ds(pl.multiple_of(H + A * c, H), A)
    f_other = pl.ds(pl.multiple_of(H + A * (1 - c), H), A)
    own = [
        pltpu.make_async_copy(a_, b_, loc.at[i])
        for i, (a_, b_) in enumerate(
            (
                (wm, wmv),
                (wm.at[:, pl.ds(pl.multiple_of(c * HC, HC), HC)], wmb.at[h, x, c]),
                (ids, idb.at[h, x, c]),
                (src, srcb.at[c]),
                (dist, distb.at[c]),
                (feats, fx.at[f_rows]),
                (wo, wov),
                (cot, cotb.at[c]),
                (radial_h, radial),
            )
        )
    ]
    for o in own:
        o.start()

    @pl.when(half == c)
    def _():
        cp = pltpu.make_async_copy(wo, wob.at[h % 2, x, c], loc.at[9])
        cp.start()
        cp.wait()

    @pl.when(q == 0)
    def _():
        fx[0:H, :] = jnp.zeros((H, C), BF16)
        rim_lo[...] = jnp.zeros((H, HC), BF16)

    @pl.when(q == 15)
    def _():
        fx[H + 2 * A :, :] = jnp.zeros((H, C), BF16)
        rim_hi[...] = jnp.zeros((H, HC), BF16)

    for o in own:
        o.wait()
    pl.semaphore_wait(bar, len(greet))

    sent = []
    other = pl.ds(pl.multiple_of((1 - c) * HC, HC), HC)
    mine_c = pl.ds(pl.multiple_of(c * HC, HC), HC)
    my_ids = idb.at[h, x, c]
    sent.append(send(my_ids, my_ids, s_iy.at[6], r_iy.at[6], partner))
    for j, hh in enumerate((hb, ha, h2)):
        for c_ in (0, 1):
            sent.append(
                send(
                    my_ids, my_ids, s_iy.at[2 * j + c_], r_iy.at[2 * j + c], dev(ylo, hh, x, c_)
                )
            )
    sent.append(send(wmv.at[:, other], wmb.at[h, x, c], s_wy.at[6], r_wy.at[6], partner))

    def wm_y(j, c_):
        yl, hh = y_to[j]
        return pltpu.make_async_remote_copy(
            src_ref=wmv.at[:, pl.ds(c_ * HC, HC)], dst_ref=wmb.at[h, x, c],
            send_sem=s_wy.at[2 * j + c_], recv_sem=r_wy.at[2 * j + c],
            device_id=dev(yl, hh, x, c_), device_id_type=MESH,
        )

    def wo_y(j):
        yl, hh = y_to[j]
        return pltpu.make_async_remote_copy(
            src_ref=wov, dst_ref=wob.at[h % 2, x, c],
            send_sem=s_oy.at[j], recv_sem=r_oy.at[2 * j + c],
            device_id=dev(yl, hh, x, half), device_id_type=MESH,
        )

    y_of = ((2,), (0, 1))
    for parity in (0, 1):
        @pl.when(par == parity)
        def _(parity=parity):
            for j in y_of[parity]:
                for c_ in (0, 1):
                    wm_y(j, c_).start()

    @pl.when(h % 2 == par)
    def _():
        for j in (2, 1, 0):
            wo_y(j).start()

    sent.append(send(srcb.at[c], srcb.at[c], s_misc.at[0], r_misc.at[0], partner))
    sent.append(send(distb.at[c], distb.at[c], s_misc.at[1], r_misc.at[1], partner))
    def wm_in(k):
        if k == 0:
            arrived(wmb.at[h, x, 1 - c], s_wy.at[6], r_wy.at[6], partner)
        else:
            for c_ in (0, 1):
                i = 2 * (k - 1) + c_
                arrived(
                    wmb.at[y_in[k - 1], x, c_], s_wy.at[i], r_wy.at[i], dev(*y_from[k - 1], x, c_)
                )

    taken = ((h + par * s + 4) % 4, (h + 2 * (1 - par) - par * s + 4) % 4)
    rest = ((h + (1 - par) * s + 4) % 4, (h + 2 * par - (1 - par) * s + 4) % 4)
    z_to = ((ylo * 8 + (z + 1) % 8, f), (ylo * 8 + (z + 7) % 8, f))
    z_in = (z_to[1], z_to[0])

    far = dev(ylo, h, x2, c)

    def wm_x(n, i):
        ref = wmb.at[taken[n], x]
        return pltpu.make_async_remote_copy(
            src_ref=ref, dst_ref=ref, send_sem=s_wx.at[n, i], recv_sem=r_wx.at[n, i],
            device_id=(right, left, far)[i], device_id_type=MESH,
        )

    def wm_z(n, i, u):
        ref = wmb.at[taken[n], (xn, xp, x2, x)[i], u]
        return pltpu.make_async_remote_copy(
            src_ref=ref, dst_ref=ref, send_sem=s_wz.at[n, i, u], recv_sem=r_wz.at[n, i, u],
            device_id=z_to[u], device_id_type=MESH,
        )

    def wm_x_start(n, parity):
        @pl.when(par == parity)
        def _():
            if n or parity:
                wm_in(3 if parity == 0 else 1 + n)
            for i in range(3):
                wm_x(n, i).start()
            if n or parity:
                for u in (0, 1):
                    wm_z(n, 3, u).start()

    def wm_x_in(n, i):
        ref = wmb.at[taken[n], (xn, xp, x2)[i]]
        arrived(ref, s_wx.at[n, i], r_wx.at[n, i], (left, right, far)[i])
        for u in (0, 1):
            wm_z(n, i, u).start()

    norm = 1.0 / math.sqrt(NB)
    PARTS = 2

    def build(p, part):
        if part == 0:
            d = distb[p]
            env = 0.5 * (jnp.cos(d * (math.pi / 5.0)) + 1.0) * norm
            for b in range(BASIS):
                bas[b] = jnp.exp(-2.0 * (d - 5.0 * b / (BASIS - 1)) ** 2) * env
        base = 2 * A * q - H + A * p

        def tile(t, carry):
            row = pl.multiple_of(t * 16, 16)
            at = row + base + lax.broadcasted_iota(jnp.int32, (16, A), 0)
            accs = [jnp.zeros((16, A), F32) for _ in range(BASIS)]
            for k in range(NB):
                hit = srcb[p, k : k + 1, :] == at
                for b in range(BASIS):
                    accs[b] = accs[b] + jnp.where(hit, bas[b, k : k + 1, :], 0.0)
            for b in range(BASIS):
                mtv[pl.ds(pl.multiple_of(b * W + row, 16), 16), :] = accs[b]
                mtc[p, pl.ds(row, 16), b * A : (b + 1) * A] = accs[b].astype(BF16)
            return carry

        step = W // 16 // PARTS
        lax.fori_loop(part * step, (part + 1) * step, tile, 0)
        if part == PARTS - 1:
            for t in range(BASIS * W // A):
                mc[p, :, t * A : (t + 1) * A] = mtv[t * A : (t + 1) * A, :].T.astype(BF16)

    wm_in(0)
    wm_x_start(0, 0)

    def wo_partner():
        return pltpu.make_async_remote_copy(
            src_ref=wov, dst_ref=wob.at[h % 2, x, c], send_sem=s_oy.at[3], recv_sem=r_oy.at[6],
            device_id=partner, device_id_type=MESH,
        )

    @pl.when(half != c)
    def _():
        wo_partner().start()

    up_ok = jnp.logical_and(c == 1, q < 15)
    dn_ok = jnp.logical_and(c == 0, q > 0)

    def up_copy(c_):
        return pltpu.make_async_remote_copy(
            src_ref=fx.at[pl.ds(2 * A, H)], dst_ref=fx.at[pl.ds(0, H)],
            send_sem=s_misc.at[4 + c_], recv_sem=r_misc.at[4],
            device_id=chip(qn, c_), device_id_type=MESH,
        )

    def dn_copy(c_):
        return pltpu.make_async_remote_copy(
            src_ref=fx.at[pl.ds(H, H)], dst_ref=fx.at[pl.ds(H + 2 * A, H)],
            send_sem=s_misc.at[4 + c_], recv_sem=r_misc.at[5],
            device_id=chip(qp, c_), device_id_type=MESH,
        )

    @pl.when(up_ok)
    def _():
        for c_ in (0, 1):
            up_copy(c_).start()

    @pl.when(dn_ok)
    def _():
        for c_ in (0, 1):
            dn_copy(c_).start()

    sent.append(send(fx.at[f_rows], fx.at[f_rows], s_misc.at[2], r_misc.at[2], partner))
    sent.append(send(cotb.at[c], cotb.at[c], s_misc.at[3], r_misc.at[3], partner))

    def wo_in():
        @pl.when(h == 2 * c + par)
        def _():
            arrived(wob.at[par, x, 1 - c], s_oy.at[3], r_oy.at[6], partner)

        for j in range(3):
            @pl.when(y_in[j] == 2 * c + par)
            def _(j=j):
                for c_ in (0, 1):
                    arrived(
                        wob.at[par, x, c_], s_oy.at[0], r_oy.at[2 * j + c_],
                        dev(*y_from[j], x, c_),
                    )

        for i, to in enumerate((right, left, far)):
            ref = wob.at[par, x]
            sent.append(send(ref, ref, s_ox.at[i], r_ox.at[i], to))

    def wo_own_z(u):
        ref = wob.at[par, x, u]
        return pltpu.make_async_remote_copy(
            src_ref=ref, dst_ref=ref, send_sem=s_oz.at[3, u], recv_sem=r_oz.at[3, u],
            device_id=z_to[u], device_id_type=MESH,
        )

    def wo_z():
        @pl.when(h != 2 * c + par)
        def _():
            for u in (0, 1):
                wo_own_z(u).start()

    def wo_x_in(i):
        col = (xn, xp, x2)[i]
        arrived(wob.at[par, col], s_ox.at[i], r_ox.at[i], (left, right, far)[i])
        for u in (0, 1):
            ref = wob.at[par, col, u]
            sent.append(send(ref, ref, s_oz.at[i, u], r_oz.at[i, u], z_to[u]))

    arrived(srcb.at[1 - c], s_misc.at[0], r_misc.at[0], partner)
    arrived(distb.at[1 - c], s_misc.at[1], r_misc.at[1], partner)
    build(0, 0)
    wm_x_start(0, 1)
    wm_x_start(1, 0)
    wm_x_start(1, 1)
    build(0, 1)
    arrived(idb.at[h, x, 1 - c], s_iy.at[6], r_iy.at[6], partner)
    for k, yb in enumerate(y_in):
        for c_ in (0, 1):
            i = 2 * k + c_
            arrived(idb.at[yb, x, c_], s_iy.at[i], r_iy.at[i], dev(ylo, yb, x, c_))
    for i, x_ in enumerate((xp, xn, x2)):
        ref = idb.at[:, x]
        sent.append(send(ref, ref, s_ix.at[i], r_ix.at[i], dev(ylo, h, x_, c)))
    wo_in()
    wm_x_in(0, 0)
    wm_x_in(0, 1)
    build(1, 0)
    wm_x_in(0, 2)
    wm_x_in(1, 1)
    wm_x_in(1, 0)
    wm_x_in(1, 2)
    build(1, 1)
    arrived(fx.at[f_other], s_misc.at[2], r_misc.at[2], partner)
    for p in (0, 1):
        feats_t[:, :, :, p * A : (p + 1) * A] = (
            fx[H + p * A : H + (p + 1) * A, :].T.reshape(4, 4, 64, A)
        )
    arrived(cotb.at[1 - c], s_misc.at[3], r_misc.at[3], partner)

    @pl.when(q > 0)
    def _():
        arrived(fx.at[pl.ds(0, H)], s_misc.at[4], r_misc.at[4], chip(qp, 1))

    @pl.when(q < 15)
    def _():
        arrived(fx.at[pl.ds(H + 2 * A, H)], s_misc.at[4], r_misc.at[5], chip(qn, 0))

    wo_z()
    wo_x_in(0)
    wo_x_in(1)
    for i, x_ in enumerate((xn, xp, x2)):
        arrived(idb.at[:, x_], s_ix.at[i], r_ix.at[i], dev(ylo, h, x_, c))
    all_ids = idb[...].reshape(32, A)
    for p in (0, 1):
        mine = idb[h, x, p]
        wrow = jnp.zeros((1, A), F32)
        for g in range(GRAPHS):
            count = jnp.sum((all_ids == g).astype(F32), axis=0, keepdims=True)
            count = jnp.sum(count, axis=1, keepdims=True)
            wrow = wrow + jnp.where(mine == g, lax.rsqrt(jnp.broadcast_to(count, (1, A))), 0.0)
        wcol = jnp.broadcast_to(wrow, (A, A)).T
        for t in range(C // A):
            cols = slice(t * A, (t + 1) * A)
            dout[p * A : (p + 1) * A, cols] = (cotb[p, :, cols].astype(F32) * wcol).astype(BF16)

    for n in (0, 1):
        for i, col in enumerate((xn, xp, x2)):
            for u in (0, 1):
                arrived(wmb.at[rest[n], col, u], s_wz.at[n, i, u], r_wz.at[n, i, u], z_in[u])
        if n:
            for u in (0, 1):
                arrived(wmb.at[rest[n], x, u], s_wz.at[n, 3, u], r_wz.at[n, 3, u], z_in[u])
        else:
            @pl.when(par == 0)
            def _():
                for u in (0, 1):
                    arrived(wmb.at[rest[0], x, u], s_wz.at[0, 3, u], r_wz.at[0, 3, u], z_in[u])

    wmat = wmb[...].reshape(C, HC)
    proj = jnp.dot(fx[...], wmat, preferred_element_type=F32).astype(BF16)
    spread[...] = proj.astype(F32)
    for p in (0, 1):
        for b in range(BASIS):
            ps[b * W : (b + 1) * W, :] = (
                spread[p * A : p * A + W, :] * radial[b : b + 1, mine_c]
            ).astype(BF16)
        agg = jnp.dot(mc[p], ps[...], preferred_element_type=F32)
        sig = 1.0 / (1.0 + jnp.exp(-agg))
        a16 = (agg * sig).astype(BF16)
        rows = slice(p * A, (p + 1) * A)
        act[rows, :] = a16
        dsl[rows, :] = sig * (1.0 + agg * (1.0 - sig))
        act_t[:, :, :, rows] = a16.T.reshape(2, 4, 64, A)

    wo_x_in(2)
    def out_part(xd):
        return jnp.dot(
            act_t[:, pl.ds(xd, 1)].reshape(A, 2 * A), dout[...], preferred_element_type=F32
        )

    v = out_part(x2)
    so[0] = v[:64].astype(BF16)
    so[1] = v[64:].astype(BF16)
    sent.append(send(so.at[0], xo.at[0], s_xo.at[0], r_xo.at[0], right))
    sent.append(send(so.at[1], xo.at[1], s_xo.at[1], r_xo.at[1], left))
    v = out_part(xp)
    ko[0] = v[:64]
    so[2] = v[64:].astype(BF16)
    sent.append(send(so.at[2], xo.at[2], s_xo.at[2], r_xo.at[2], right))
    v = out_part(xn)
    so[3] = v[:64].astype(BF16)
    ko[1] = v[64:]
    sent.append(send(so.at[3], xo.at[3], s_xo.at[3], r_xo.at[3], left))
    v = out_part(x)
    ko[2] = v[:64]
    ko[3] = v[64:]

    for i, x_ in enumerate((xn, xp, x2)):
        for u in (0, 1):
            arrived(wob.at[1 - par, x_, u], s_oz.at[i, u], r_oz.at[i, u], z_in[u])

    @pl.when(h != 2 * c + 1 - par)
    def _():
        for u in (0, 1):
            arrived(wob.at[1 - par, x, u], s_oz.at[3, u], r_oz.at[3, u], z_in[u])

    @pl.when(h == 2 * c + 1 - par)
    def _():
        arrived(wob.at[1 - par, x, 1 - c], s_oy.at[3], r_oy.at[6], partner)

    womat = wob[...].reshape(HC, C)
    for p in (0, 1):
        rows = slice(p * A, (p + 1) * A)
        dagg = contract(dout[rows, :], womat, 1, 1) * dsl[rows, :]
        for b in range(BASIS):
            rr[b * A : (b + 1) * A, :] = (dagg * radial[b : b + 1, mine_c]).astype(BF16)
        part = jnp.dot(mtc[p], rr[...], preferred_element_type=F32)
        if p == 0:
            spread[0:W, :] = part
            rim_s[0] = part[:H].astype(BF16)
        else:
            spread[A:W, :] = spread[A:W, :] + part[: W - A]
            spread[W:, :] = part[W - A :]
            rim_s[1] = part[W - H :].astype(BF16)

    def rim_dn():
        return pltpu.make_async_remote_copy(
            src_ref=rim_s.at[0], dst_ref=rim_hi, send_sem=s_misc.at[6], recv_sem=r_misc.at[6],
            device_id=chip(qp, c), device_id_type=MESH,
        )

    def rim_up():
        return pltpu.make_async_remote_copy(
            src_ref=rim_s.at[1], dst_ref=rim_lo, send_sem=s_misc.at[7], recv_sem=r_misc.at[7],
            device_id=chip(qn, c), device_id_type=MESH,
        )

    @pl.when(q > 0)
    def _():
        rim_dn().start()

    @pl.when(q < 15)
    def _():
        rim_up().start()

    arrived(xo.at[0], s_xo.at[0], r_xo.at[0], left)
    so[4] = (ko[0] + xo[0].astype(F32)).astype(BF16)
    sent.append(send(so.at[4], xo.at[4], s_xo.at[4], r_xo.at[4], right))
    arrived(xo.at[1], s_xo.at[1], r_xo.at[1], right)
    so[5] = (ko[1] + xo[1].astype(F32)).astype(BF16)
    sent.append(send(so.at[5], xo.at[5], s_xo.at[5], r_xo.at[5], left))

    @pl.when(q > 0)
    def _():
        arrived(rim_lo, s_misc.at[7], r_misc.at[7], chip(qp, c))

    @pl.when(q < 15)
    def _():
        arrived(rim_hi, s_misc.at[6], r_misc.at[6], chip(qn, c))

    spread[H : 2 * H, :] = spread[H : 2 * H, :] + rim_lo[...].astype(F32)
    spread[2 * A : 2 * A + H, :] = spread[2 * A : 2 * A + H, :] + rim_hi[...].astype(F32)

    def turned(rows, back, blocks):
        which = jnp.full((rows, FRAG), frag[0], jnp.int32)
        res = []
        for k in range(4):
            v_ = blocks(k)
            for o in range(1, 4):
                hit = jnp.logical_or(which == o, which == o + 4)
                v_ = jnp.where(hit, blocks((k - o if back else k + o) % 4), v_)
            res.append(v_)
        return res

    for k, v in enumerate(
        turned(2 * A, False, lambda k: spread[H : H + 2 * A, k * FRAG : (k + 1) * FRAG])
    ):
        dproj[:, k * FRAG : (k + 1) * FRAG] = v.astype(BF16)

    def msg_part(xd, store_lo, store_hi):
        v_ = jnp.dot(
            feats_t[:, pl.ds(xd, 1)].reshape(2 * A, 2 * A), dproj[...], preferred_element_type=F32
        )
        for k in range(4):
            store_lo(k, v_[:A, k * FRAG : (k + 1) * FRAG])
            store_hi(k, v_[A:, k * FRAG : (k + 1) * FRAG])

    def staged(i):
        def f_(k, v_):
            sm[k, i] = v_.astype(BF16)
        return f_

    def kept(i):
        def f_(k, v_):
            km[k, i] = v_
        return f_

    msg_part(x2, staged(0), staged(1))
    msg_part(xp, kept(0), staged(2))
    msg_part(xn, staged(3), kept(1))
    msg_part(x, kept(2), kept(3))

    def msg_leg(k, i):
        to = (right, left, right, left, right, left)[i]
        send(sm.at[k, i], xm.at[k, i], s_xm.at[0], r_xm.at[k, 0 if i < 2 else 1], to)

    def msg_first(k):
        for i in range(4):
            msg_leg(k, i)

    def msg_relay(k):
        both(xm.at[k, pl.ds(0, 2)], s_xm.at[0], r_xm.at[k, 0]).wait_recv()
        for i in (0, 1):
            sm[k, 4 + i] = (km[k, i] + xm[k, i].astype(F32)).astype(BF16)
            msg_leg(k, 4 + i)

    def msg_y(k):
        both(xm.at[k, pl.ds(2, 4)], s_xm.at[0], r_xm.at[k, 1]).wait_recv()
        lo = (km[k, 2] + xm[k, 3].astype(F32) + xm[k, 4].astype(F32)).astype(BF16)
        hi = (km[k, 3] + xm[k, 2].astype(F32) + xm[k, 5].astype(F32)).astype(BF16)
        sym[k, 0:2] = lo.reshape(2, 2, 32, FRAG)
        sym[k, 2:4] = hi.reshape(2, 2, 32, FRAG)
        for d in (5, 4, 7, 6, 3, 2, 1):
            hh, c_ = (h + d // 2) % 4, (c + d) % 2
            send(
                sym.at[k, hh, c_], ym.at[k, 2 * h + c], s_ym.at[k], r_ym.at[k],
                dev(ylo, hh, x, c_),
            )
        ym[k, 2 * h + c] = sym[k, h, c]

    def msg_sum(k):
        both(ym.at[k, pl.ds(0, 7)], s_ym.at[k], r_ym.at[k]).wait_recv()
        for c_ in (0, 1):
            gm[c_, k] = (
                ym[k, c_].astype(F32) + ym[k, 2 + c_].astype(F32)
                + ym[k, 4 + c_].astype(F32) + ym[k, 6 + c_].astype(F32)
            )

    msg_first(0)
    msg_first(1)

    arrived(xo.at[3], s_xo.at[3], r_xo.at[3], right)
    arrived(xo.at[4], s_xo.at[4], r_xo.at[4], left)
    arrived(xo.at[2], s_xo.at[2], r_xo.at[2], left)
    arrived(xo.at[5], s_xo.at[5], r_xo.at[5], right)
    syo[0] = (ko[2] + xo[3].astype(F32) + xo[4].astype(F32)).astype(BF16).reshape(2, 32, C)
    syo[1] = (ko[3] + xo[2].astype(F32) + xo[5].astype(F32)).astype(BF16).reshape(2, 32, C)

    def yo_copy(e, c_):
        return pltpu.make_async_remote_copy(
            src_ref=syo.at[e, c_], dst_ref=yo.at[h],
            send_sem=s_yo.at[2 * e + c_], recv_sem=r_yo.at[h],
            device_id=dev(ylo, 2 * c + e, x, c_), device_id_type=MESH,
        )

    for e in (0, 1):
        for c_ in (0, 1):
            is_me = jnp.logical_and(2 * c + e == h, c == c_)

            @pl.when(jnp.logical_not(is_me))
            def _(e=e, c_=c_):
                yo_copy(e, c_).start()

            @pl.when(is_me)
            def _(e=e, c_=c_):
                cp = pltpu.make_async_copy(syo.at[e, c_], yo.at[h], loc.at[7])
                cp.start()
                cp.wait()

    womat = wob[...].reshape(HC, C)
    a_other = act[pl.ds(pl.multiple_of((1 - c) * A, A), A), :]
    part_s[...] = jnp.dot(a_other, womat, preferred_element_type=F32).astype(BF16)
    sent.append(send(part_s, part_r, s_misc.at[8], r_misc.at[8], partner))
    a_own = act[pl.ds(pl.multiple_of(c * A, A), A), :]
    node_own = jnp.dot(a_own, womat, preferred_element_type=F32) + fx[f_rows, :].astype(F32)

    msg_relay(0)
    msg_first(2)
    msg_relay(1)
    msg_first(3)
    msg_y(0)
    msg_relay(2)
    msg_y(1)
    msg_relay(3)
    for h_ in range(4):
        @pl.when(jnp.logical_or(h_ != h, c != half))
        def _(h_=h_):
            arrived(yo.at[h_], s_yo.at[0], r_yo.at[h_], dev(ylo, h_, x, half))

    total = yo[0].astype(F32) + yo[1].astype(F32) + yo[2].astype(F32) + yo[3].astype(F32)
    gout_o[0] = total.astype(BF16)
    put(2, gout_o, gout_h)
    gf[...] = total
    chosen = jnp.full((32, FRAG), frag[0], jnp.int32)

    def decoded(piece):
        scale = (jnp.max(jnp.abs(piece), axis=1, keepdims=True) + TINY).astype(BF16).astype(F32)
        code = (piece / scale).astype(BF16).astype(F32)
        return (scale * code).astype(BF16)

    peers = sorted(
        ((dy, dz) for dy in range(2) for dz in range(8) if dy or dz),
        key=lambda p_: -(p_[0] + min(p_[1], 8 - p_[1])),
    )

    def outer_send(m, buf, ss, rs):
        for dy, dz in peers:
            to = ((ylo + dy) % 2 * 8 + (z + dz) % 8, f)
            send(tb.at[m], buf.at[r], ss.at[0], rs.at[0], to)

    def outer_sum(m, buf, ss, rs):
        both(buf.at[pl.ds(0, 15)], ss.at[0], rs.at[0]).wait_recv()
        outer_o[m] = jnp.sum(buf[...].astype(F32), axis=0)

    piece = jnp.zeros((32, FRAG), F32)
    for b in range(C // FRAG):
        piece = jnp.where(chosen == b, gf[:, b * FRAG : (b + 1) * FRAG], piece)
    term = decoded(piece)
    tb[1] = term
    oo[r] = term
    outer_send(1, oo, s_oo, r_oo)

    msg_y(2)
    msg_y(3)
    msg_sum(0)
    term = decoded(jnp.where(chosen < 4, gm[0, 0], gm[1, 0]))
    tb[0] = term
    om[r] = term
    outer_send(0, om, s_om, r_om)
    arrived(part_r, s_misc.at[8], r_misc.at[8], partner)
    node_o[...] = (node_own + part_r[...].astype(F32)).astype(BF16)
    put(0, node_o, node_h)
    outer_sum(1, oo, s_oo, r_oo)
    for k in (1, 2, 3):
        msg_sum(k)
    for c_ in (0, 1):
        for k, v in enumerate(turned(32, True, lambda k: gm[c_, k])):
            gmsg_o[0, :, c_ * HC + k * FRAG : c_ * HC + (k + 1) * FRAG] = v.astype(BF16)
    put(1, gmsg_o, gmsg_h)
    outer_sum(0, om, s_om, r_om)
    put(3, outer_o, outer_h)

    for cp in puts:
        cp.wait()
    both(sm, s_xm.at[0], s_xm.at[0]).wait_send()
    for k in range(4):
        both(ym.at[k, pl.ds(0, 7)], s_ym.at[k], r_ym.at[k]).wait_send()
    both(oo.at[pl.ds(0, 15)], s_oo.at[0], r_oo.at[0]).wait_send()
    both(om.at[pl.ds(0, 15)], s_om.at[0], r_om.at[0]).wait_send()
    for cp in sent:
        cp.wait_send()

    @pl.when(up_ok)
    def _():
        for c_ in (0, 1):
            up_copy(c_).wait_send()

    @pl.when(dn_ok)
    def _():
        for c_ in (0, 1):
            dn_copy(c_).wait_send()

    @pl.when(half != c)
    def _():
        wo_partner().wait_send()

    for n in (0, 1):
        for i in range(3):
            wm_x(n, i).wait_send()
        for i in range(3):
            for u in (0, 1):
                wm_z(n, i, u).wait_send()
    for u in (0, 1):
        wm_z(1, 3, u).wait_send()

    for parity in (0, 1):
        @pl.when(par == parity)
        def _(parity=parity):
            for j in y_of[parity]:
                for c_ in (0, 1):
                    wm_y(j, c_).wait_send()
            if parity:
                for u in (0, 1):
                    wm_z(0, 3, u).wait_send()

    @pl.when(h % 2 == par)
    def _():
        for j in range(3):
            wo_y(j).wait_send()

    @pl.when(h != 2 * c + par)
    def _():
        for u in (0, 1):
            wo_own_z(u).wait_send()
    @pl.when(q > 0)
    def _():
        rim_dn().wait_send()

    @pl.when(q < 15)
    def _():
        rim_up().wait_send()

    for e in (0, 1):
        for c_ in (0, 1):
            @pl.when(jnp.logical_not(jnp.logical_and(2 * c + e == h, c == c_)))
            def _(e=e, c_=c_):
                yo_copy(e, c_).wait_send()


def finish(*refs):
    sems = refs[8]
    copies = [pltpu.make_async_copy(refs[i], refs[4 + i], sems.at[i]) for i in range(4)]
    for cp in copies:
        cp.start()
    for cp in copies:
        cp.wait()


def shards(feats, src, dist, ids, wm, wo, radial, cot, frag):
    vm = pl.BlockSpec(memory_space=pltpu.VMEM)
    dma = lambda *n: pltpu.SemaphoreType.DMA(n)
    V = pltpu.VMEM
    results = pl.pallas_call(
        body,
        out_shape=(
            jax.ShapeDtypeStruct((A, C), BF16),
            jax.ShapeDtypeStruct((1, 32, C), BF16),
            jax.ShapeDtypeStruct((1, 32, C), BF16),
            jax.ShapeDtypeStruct((2, 32, FRAG), F32),
        ),
        in_specs=[pl.BlockSpec(memory_space=pl.ANY)] * 8 + [pl.BlockSpec(memory_space=pltpu.SMEM)],
        out_specs=(pl.BlockSpec(memory_space=pl.ANY),) * 4,
        scratch_shapes=[
            V((4, 4, 2, 32, HC), BF16),
            V((2, 4, 2, 32, C), BF16),
            V((32, C), BF16),
            V((32, C), BF16),
            V((BASIS, C), F32),
            V((4, 4, 2, 1, A), jnp.int32),
            V((EXT, C), BF16),
            V((2, A, C), BF16),
            V((2, NB, A), jnp.int32),
            V((2, NB, A), F32),
            V((A, C), BF16),
            V((H, HC), BF16),
            V((H, HC), BF16),
            V((6, 64, C), BF16),
            V((4, 6, A, FRAG), BF16),
            V((4, 32, C), BF16),
            V((4, 8, 32, FRAG), BF16),
            V((16, 32, FRAG), BF16),
            V((16, 32, FRAG), BF16),
            V((BASIS, NB, A), F32),
            V((BASIS * W, A), F32),
            V((2, W, BASIS * A), BF16),
            V((2, A, BASIS * W), BF16),
            V((BASIS * W, HC), BF16),
            V((2 * A, HC), BF16),
            V((2 * A, HC), F32),
            V((2, 4, 64, 2 * A), BF16),
            V((4, 4, 64, 2 * A), BF16),
            V((2 * A, C), BF16),
            V((BASIS * A, HC), BF16),
            V((EXT, HC), F32),
            V((2 * A, HC), BF16),
            V((A, C), BF16),
            V((2, H, HC), BF16),
            V((6, 64, C), BF16),
            V((4, 64, C), F32),
            V((4, 6, A, FRAG), BF16),
            V((4, 4, A, FRAG), F32),
            V((2, 2, 32, C), BF16),
            V((4, 4, 2, 32, FRAG), BF16),
            V((32, C), F32),
            V((2, 4, 32, FRAG), F32),
            V((2, 32, FRAG), BF16),
            V((A, C), BF16),
            V((1, 32, C), BF16),
            V((1, 32, C), BF16),
            V((2, 32, FRAG), F32),
            dma(14),
            dma(7), dma(7), dma(7), dma(7), dma(4), dma(7),
            dma(2, 3), dma(2, 3), dma(2, 4, 2), dma(2, 4, 2), dma(3), dma(3),
            dma(4), dma(4), dma(4, 2), dma(4, 2),
            dma(9), dma(9), dma(6), dma(6), dma(1), dma(4, 2),
            dma(4), dma(4), dma(4), dma(4), dma(1), dma(1), dma(1), dma(1),
        ],
        compiler_params=pltpu.CompilerParams(
            collective_id=0, has_side_effects=True, vmem_limit_bytes=56 << 20
        ),
        name="step",
    )(feats, src, dist, ids, wm, wo, radial, cot, frag)
    anywhere = pl.BlockSpec(memory_space=pl.ANY)
    return pl.pallas_call(
        finish,
        out_shape=tuple(jax.ShapeDtypeStruct(v.shape, v.dtype) for v in results),
        in_specs=[vm] * 4,
        out_specs=(anywhere,) * 4,
        scratch_shapes=[dma(4)],
        compiler_params=pltpu.CompilerParams(vmem_limit_bytes=60 << 20),
        name="finish",
    )(*results)


def solution(mesh):
    placed = (
        P(("replica", "fsdp"), None),
        P(None, ("replica", "fsdp")),
        P(None, ("replica", "fsdp")),
        P("replica", "fsdp"),
        P("fsdp", None),
        P("fsdp", None),
        P(),
        P(("replica", "fsdp"), None),
        P(),
    )
    return jax.shard_map(
        shards,
        mesh=mesh,
        in_specs=placed,
        out_specs=(
            P(("replica", "fsdp"), None),
            P("replica", "fsdp", None),
            P("replica", "fsdp", None),
            P(None, "fsdp", None),
        ),
        check_vma=False,
    )
```

```python
import functools
import math

import jax
import jax.numpy as jnp
from jax import lax
from jax.experimental import pallas as pl
from jax.experimental.pallas import tpu as pltpu
from jax.sharding import PartitionSpec as P

MESH = pl.DeviceIdType.MESH
F32 = jnp.float32
BF16 = jnp.bfloat16
GRAPHS = 8
FRAG = 128
A = 128
C = 1024
HC = 512
H = 32
NB = 12
BASIS = 8
W = 2 * A - 64
EXT = 2 * A + 2 * H
TINY = 1e-6


def contract(a, b, da, db):
    return lax.dot_general(a, b, (((da,), (db,)), ((), ())), preferred_element_type=F32)


def body(
    feats, src, dist, ids, wm, wo, radial_h, cot, frag,
    node_h, gmsg_h, gout_h, outer_h,
    wmb, wob, wmv, wov, radial, idb, fx, cotb, srcb, distb, part_r,
    rim_lo, rim_hi, xo, xm, yo, ym, oo, om,
    bas, mtv, mtc, mc, ps, act, dsl, act_t, feats_t, dout, rr, spread, dproj,
    part_s, rim_s, so, ko, sm, km, syo, sym, gf, gm, tb, node_o, gmsg_o, gout_o, outer_o,
    loc, s_wy, r_wy, s_iy, r_iy, s_oy, r_oy, s_wx, r_wx, s_wz, r_wz, s_ix, r_ix,
    s_ox, r_ox, s_oz, r_oz,
    s_misc, r_misc, s_xo, r_xo, s_xm, r_xm, s_yo, r_yo, s_ym, r_ym, s_oo, r_oo, s_om, r_om,
):
    r = lax.axis_index("replica")
    f = lax.axis_index("fsdp")
    ylo, z = r // 8, r % 8
    h, x, c = f // 8, (f // 2) % 4, f % 2
    q = f // 2
    s = 2 * ylo - 1
    xp, xn, x2 = (x + 1) % 4, (x + 3) % 4, (x + 2) % 4
    ha, hb, h2 = (h + s + 4) % 4, (h - s + 4) % 4, (h + 2) % 4
    half = h // 2
    par = z % 2

    def dev(ylo_, h_, x_, c_):
        return (ylo_ * 8 + z, h_ * 8 + x_ * 2 + c_)

    def chip(q_, c_):
        return (r, q_ * 2 + c_)

    partner = dev(ylo, h, x, 1 - c)
    right, left = dev(ylo, h, xp, c), dev(ylo, h, xn, c)
    qn, qp = (q + 1) % 16, (q + 15) % 16
    y_to = ((1 - ylo, ha), (ylo, ha), (1 - ylo, h2))
    y_in = (ha, hb, h2)
    y_from = ((1 - ylo, ha), (ylo, hb), (1 - ylo, h2))

    def send(a_, b_, ss, rs, to):
        cp = pltpu.make_async_remote_copy(
            src_ref=a_, dst_ref=b_, send_sem=ss, recv_sem=rs, device_id=to, device_id_type=MESH
        )
        cp.start()
        return cp

    def arrived(b_, ss, rs, frm):
        pltpu.make_async_remote_copy(
            src_ref=b_, dst_ref=b_, send_sem=ss, recv_sem=rs, device_id=frm, device_id_type=MESH
        ).wait_recv()

    def put(i, a_, b_):
        cp = pltpu.make_async_copy(a_, b_, loc.at[10 + i])
        cp.start()
        puts.append(cp)

    puts = []
    def both(ref, ss, rs):
        return pltpu.make_async_remote_copy(
            src_ref=ref, dst_ref=ref, send_sem=ss, recv_sem=rs, device_id=partner,
            device_id_type=MESH,
        )

    bar = pltpu.get_barrier_semaphore()
    greet = [partner]
    for c_ in (0, 1):
        greet += [dev(ylo, h, x_, c_) for x_ in (xp, xn, x2)]
        greet += [
            dev(ylo, ha, x, c_), dev(ylo, hb, x, c_), dev(ylo, h2, x, c_),
            dev(1 - ylo, ha, x, c_), dev(1 - ylo, h2, x, c_), chip(qn, c_), chip(qp, c_),
        ]
    greet += [((r + d) % 16, f) for d in range(1, 16)]
    for g in greet:
        pl.semaphore_signal(bar, inc=1, device_id=g, device_id_type=MESH)

    f_rows = pl.ds(pl.multiple_of(H + A * c, H), A)
    f_other = pl.ds(pl.multiple_of(H + A * (1 - c), H), A)
    own = [
        pltpu.make_async_copy(a_, b_, loc.at[i])
        for i, (a_, b_) in enumerate(
            (
                (wm, wmv),
                (wm.at[:, pl.ds(pl.multiple_of(c * HC, HC), HC)], wmb.at[h, x, c]),
                (ids, idb.at[h, x, c]),
                (src, srcb.at[c]),
                (dist, distb.at[c]),
                (feats, fx.at[f_rows]),
                (wo, wov),
                (cot, cotb.at[c]),
                (radial_h, radial),
            )
        )
    ]
    for o in own:
        o.start()

    @pl.when(half == c)
    def _():
        cp = pltpu.make_async_copy(wo, wob.at[h % 2, x, c], loc.at[9])
        cp.start()
        cp.wait()

    @pl.when(q == 0)
    def _():
        fx[0:H, :] = jnp.zeros((H, C), BF16)
        rim_lo[...] = jnp.zeros((H, HC), BF16)

    @pl.when(q == 15)
    def _():
        fx[H + 2 * A :, :] = jnp.zeros((H, C), BF16)
        rim_hi[...] = jnp.zeros((H, HC), BF16)

    for o in own:
        o.wait()
    pl.semaphore_wait(bar, len(greet))

    sent = []
    other = pl.ds(pl.multiple_of((1 - c) * HC, HC), HC)
    mine_c = pl.ds(pl.multiple_of(c * HC, HC), HC)
    my_ids = idb.at[h, x, c]
    sent.append(send(my_ids, my_ids, s_iy.at[6], r_iy.at[6], partner))
    for j, hh in enumerate((hb, ha, h2)):
        for c_ in (0, 1):
            sent.append(
                send(
                    my_ids, my_ids, s_iy.at[2 * j + c_], r_iy.at[2 * j + c], dev(ylo, hh, x, c_)
                )
            )
    sent.append(send(wmv.at[:, other], wmb.at[h, x, c], s_wy.at[6], r_wy.at[6], partner))

    def wm_y(j, c_):
        yl, hh = y_to[j]
        return pltpu.make_async_remote_copy(
            src_ref=wmv.at[:, pl.ds(c_ * HC, HC)], dst_ref=wmb.at[h, x, c],
            send_sem=s_wy.at[2 * j + c_], recv_sem=r_wy.at[2 * j + c],
            device_id=dev(yl, hh, x, c_), device_id_type=MESH,
        )

    def wo_y(j):
        yl, hh = y_to[j]
        return pltpu.make_async_remote_copy(
            src_ref=wov, dst_ref=wob.at[h % 2, x, c],
            send_sem=s_oy.at[j], recv_sem=r_oy.at[2 * j + c],
            device_id=dev(yl, hh, x, half), device_id_type=MESH,
        )

    y_of = ((2,), (0, 1))
    for parity in (0, 1):
        @pl.when(par == parity)
        def _(parity=parity):
            for j in y_of[parity]:
                for c_ in (0, 1):
                    wm_y(j, c_).start()

    @pl.when(h % 2 == par)
    def _():
        for j in (2, 1, 0):
            wo_y(j).start()

    sent.append(send(srcb.at[c], srcb.at[c], s_misc.at[0], r_misc.at[0], partner))
    sent.append(send(distb.at[c], distb.at[c], s_misc.at[1], r_misc.at[1], partner))
    def wm_in(k):
        if k == 0:
            arrived(wmb.at[h, x, 1 - c], s_wy.at[6], r_wy.at[6], partner)
        else:
            for c_ in (0, 1):
                i = 2 * (k - 1) + c_
                arrived(
                    wmb.at[y_in[k - 1], x, c_], s_wy.at[i], r_wy.at[i], dev(*y_from[k - 1], x, c_)
                )

    taken = ((h + par * s + 4) % 4, (h + 2 * (1 - par) - par * s + 4) % 4)
    rest = ((h + (1 - par) * s + 4) % 4, (h + 2 * par - (1 - par) * s + 4) % 4)
    z_to = ((ylo * 8 + (z + 1) % 8, f), (ylo * 8 + (z + 7) % 8, f))
    z_in = (z_to[1], z_to[0])

    far = dev(ylo, h, x2, c)

    def wm_x(n, i):
        ref = wmb.at[taken[n], x]
        return pltpu.make_async_remote_copy(
            src_ref=ref, dst_ref=ref, send_sem=s_wx.at[n], recv_sem=r_wx.at[n, i],
            device_id=(right, left, far)[i], device_id_type=MESH,
        )

    def wm_z(n, i, u):
        ref = wmb.at[taken[n], (xn, xp, x2, x)[i], u]
        return pltpu.make_async_remote_copy(
            src_ref=ref, dst_ref=ref, send_sem=s_wz.at[n], recv_sem=r_wz.at[n],
            device_id=z_to[u], device_id_type=MESH,
        )

    def wm_x_start(n, parity):
        @pl.when(par == parity)
        def _():
            if n or parity:
                wm_in(3 if parity == 0 else 1 + n)
            for i in range(3):
                wm_x(n, i).start()
            if n or parity:
                for u in (0, 1):
                    wm_z(n, 3, u).start()

    def wm_x_in(n, i):
        ref = wmb.at[taken[n], (xn, xp, x2)[i]]
        arrived(ref, s_wx.at[n], r_wx.at[n, i], (left, right, far)[i])
        for u in (0, 1):
            wm_z(n, i, u).start()

    norm = 1.0 / math.sqrt(NB)
    PARTS = 2

    def build(p, part):
        if part == 0:
            d = distb[p]
            env = 0.5 * (jnp.cos(d * (math.pi / 5.0)) + 1.0) * norm
            for b in range(BASIS):
                bas[b] = jnp.exp(-2.0 * (d - 5.0 * b / (BASIS - 1)) ** 2) * env
        base = 2 * A * q - H + A * p

        def tile(t, carry):
            row = pl.multiple_of(t * 16, 16)
            at = row + base + lax.broadcasted_iota(jnp.int32, (16, A), 0)
            accs = [jnp.zeros((16, A), F32) for _ in range(BASIS)]
            for k in range(NB):
                hit = srcb[p, k : k + 1, :] == at
                for b in range(BASIS):
                    accs[b] = accs[b] + jnp.where(hit, bas[b, k : k + 1, :], 0.0)
            for b in range(BASIS):
                mtv[pl.ds(pl.multiple_of(b * W + row, 16), 16), :] = accs[b]
                mtc[p, pl.ds(row, 16), b * A : (b + 1) * A] = accs[b].astype(BF16)
            return carry

        step = W // 16 // PARTS
        lax.fori_loop(part * step, (part + 1) * step, tile, 0)
        if part == PARTS - 1:
            for t in range(BASIS * W // A):
                mc[p, :, t * A : (t + 1) * A] = mtv[t * A : (t + 1) * A, :].T.astype(BF16)

    wm_in(0)
    wm_x_start(0, 0)

    def wo_partner():
        return pltpu.make_async_remote_copy(
            src_ref=wov, dst_ref=wob.at[h % 2, x, c], send_sem=s_oy.at[3], recv_sem=r_oy.at[6],
            device_id=partner, device_id_type=MESH,
        )

    @pl.when(half != c)
    def _():
        wo_partner().start()

    up_ok = jnp.logical_and(c == 1, q < 15)
    dn_ok = jnp.logical_and(c == 0, q > 0)

    def up_copy(c_):
        return pltpu.make_async_remote_copy(
            src_ref=fx.at[pl.ds(2 * A, H)], dst_ref=fx.at[pl.ds(0, H)],
            send_sem=s_misc.at[4 + c_], recv_sem=r_misc.at[4],
            device_id=chip(qn, c_), device_id_type=MESH,
        )

    def dn_copy(c_):
        return pltpu.make_async_remote_copy(
            src_ref=fx.at[pl.ds(H, H)], dst_ref=fx.at[pl.ds(H + 2 * A, H)],
            send_sem=s_misc.at[4 + c_], recv_sem=r_misc.at[5],
            device_id=chip(qp, c_), device_id_type=MESH,
        )

    @pl.when(up_ok)
    def _():
        for c_ in (0, 1):
            up_copy(c_).start()

    @pl.when(dn_ok)
    def _():
        for c_ in (0, 1):
            dn_copy(c_).start()

    sent.append(send(fx.at[f_rows], fx.at[f_rows], s_misc.at[2], r_misc.at[2], partner))
    sent.append(send(cotb.at[c], cotb.at[c], s_misc.at[3], r_misc.at[3], partner))

    def wo_in():
        @pl.when(h == 2 * c + par)
        def _():
            arrived(wob.at[par, x, 1 - c], s_oy.at[3], r_oy.at[6], partner)

        for j in range(3):
            @pl.when(y_in[j] == 2 * c + par)
            def _(j=j):
                for c_ in (0, 1):
                    arrived(
                        wob.at[par, x, c_], s_oy.at[0], r_oy.at[2 * j + c_],
                        dev(*y_from[j], x, c_),
                    )

        for i, to in enumerate((right, left, far)):
            ref = wob.at[par, x]
            sent.append(send(ref, ref, s_ox.at[i], r_ox.at[i], to))

    def wo_own_z(u):
        ref = wob.at[par, x, u]
        return pltpu.make_async_remote_copy(
            src_ref=ref, dst_ref=ref, send_sem=s_oz.at[0], recv_sem=r_oz.at[0],
            device_id=z_to[u], device_id_type=MESH,
        )

    def wo_z():
        @pl.when(h != 2 * c + par)
        def _():
            for u in (0, 1):
                wo_own_z(u).start()

    def wo_x_in(i):
        col = (xn, xp, x2)[i]
        arrived(wob.at[par, col], s_ox.at[i], r_ox.at[i], (left, right, far)[i])
        for u in (0, 1):
            ref = wob.at[par, col, u]
            send(ref, ref, s_oz.at[0], r_oz.at[0], z_to[u])

    arrived(srcb.at[1 - c], s_misc.at[0], r_misc.at[0], partner)
    arrived(distb.at[1 - c], s_misc.at[1], r_misc.at[1], partner)
    build(0, 0)
    wm_x_start(0, 1)
    wm_x_start(1, 0)
    wm_x_start(1, 1)
    build(0, 1)
    arrived(idb.at[h, x, 1 - c], s_iy.at[6], r_iy.at[6], partner)
    for k, yb in enumerate(y_in):
        for c_ in (0, 1):
            i = 2 * k + c_
            arrived(idb.at[yb, x, c_], s_iy.at[i], r_iy.at[i], dev(ylo, yb, x, c_))
    for i, x_ in enumerate((xp, xn, x2)):
        ref = idb.at[:, x]
        send(ref, ref, s_ix.at[0], r_ix.at[0], dev(ylo, h, x_, c))
    wm_x_in(0, 0)
    wm_x_in(0, 1)
    wo_in()
    build(1, 0)
    wm_x_in(0, 2)
    wm_x_in(1, 1)
    wm_x_in(1, 0)
    wm_x_in(1, 2)
    build(1, 1)
    arrived(fx.at[f_other], s_misc.at[2], r_misc.at[2], partner)
    for p in (0, 1):
        feats_t[:, :, :, p * A : (p + 1) * A] = (
            fx[H + p * A : H + (p + 1) * A, :].T.reshape(4, 4, 64, A)
        )
    arrived(cotb.at[1 - c], s_misc.at[3], r_misc.at[3], partner)

    @pl.when(q > 0)
    def _():
        arrived(fx.at[pl.ds(0, H)], s_misc.at[4], r_misc.at[4], chip(qp, 1))

    @pl.when(q < 15)
    def _():
        arrived(fx.at[pl.ds(H + 2 * A, H)], s_misc.at[4], r_misc.at[5], chip(qn, 0))

    wo_z()
    wo_x_in(0)
    wo_x_in(1)
    both(idb.at[pl.ds(0, 3)], s_ix.at[0], r_ix.at[0]).wait_recv()
    all_ids = idb[...].reshape(32, A)
    for p in (0, 1):
        mine = idb[h, x, p]
        wrow = jnp.zeros((1, A), F32)
        for g in range(GRAPHS):
            count = jnp.sum((all_ids == g).astype(F32), axis=0, keepdims=True)
            count = jnp.sum(count, axis=1, keepdims=True)
            wrow = wrow + jnp.where(mine == g, lax.rsqrt(jnp.broadcast_to(count, (1, A))), 0.0)
        wcol = jnp.broadcast_to(wrow, (A, A)).T
        for t in range(C // A):
            cols = slice(t * A, (t + 1) * A)
            dout[p * A : (p + 1) * A, cols] = (cotb[p, :, cols].astype(F32) * wcol).astype(BF16)

    both(wmb.at[0], s_wz.at[1], r_wz.at[1]).wait_recv()
    for parity in (0, 1):
        @pl.when(par == parity)
        def _(parity=parity):
            ref = wmb.at[0, pl.ds(0, 3)] if parity else wmb.at[0]
            both(ref, s_wz.at[0], r_wz.at[0]).wait_recv()

    wmat = wmb[...].reshape(C, HC)
    proj = jnp.dot(fx[...], wmat, preferred_element_type=F32).astype(BF16)
    spread[...] = proj.astype(F32)
    for p in (0, 1):
        for b in range(BASIS):
            ps[b * W : (b + 1) * W, :] = (
                spread[p * A : p * A + W, :] * radial[b : b + 1, mine_c]
            ).astype(BF16)
        agg = jnp.dot(mc[p], ps[...], preferred_element_type=F32)
        sig = 1.0 / (1.0 + jnp.exp(-agg))
        a16 = (agg * sig).astype(BF16)
        rows = slice(p * A, (p + 1) * A)
        act[rows, :] = a16
        dsl[rows, :] = sig * (1.0 + agg * (1.0 - sig))
        act_t[:, :, :, rows] = a16.T.reshape(2, 4, 64, A)

    wo_x_in(2)
    def out_part(xd):
        return jnp.dot(
            act_t[:, pl.ds(xd, 1)].reshape(A, 2 * A), dout[...], preferred_element_type=F32
        )

    v = out_part(x2)
    so[0] = v[:64].astype(BF16)
    so[1] = v[64:].astype(BF16)
    sent.append(send(so.at[0], xo.at[0], s_xo.at[0], r_xo.at[0], right))
    sent.append(send(so.at[1], xo.at[1], s_xo.at[1], r_xo.at[1], left))
    v = out_part(xp)
    ko[0] = v[:64]
    so[2] = v[64:].astype(BF16)
    sent.append(send(so.at[2], xo.at[2], s_xo.at[2], r_xo.at[2], right))
    v = out_part(xn)
    so[3] = v[:64].astype(BF16)
    ko[1] = v[64:]
    sent.append(send(so.at[3], xo.at[3], s_xo.at[3], r_xo.at[3], left))
    v = out_part(x)
    ko[2] = v[:64]
    ko[3] = v[64:]

    @pl.when(h != 2 * c + 1 - par)
    def _():
        both(wob.at[0], s_oz.at[0], r_oz.at[0]).wait_recv()

    @pl.when(h == 2 * c + 1 - par)
    def _():
        both(wob.at[0, pl.ds(0, 3)], s_oz.at[0], r_oz.at[0]).wait_recv()

    @pl.when(h == 2 * c + 1 - par)
    def _():
        arrived(wob.at[1 - par, x, 1 - c], s_oy.at[3], r_oy.at[6], partner)

    womat = wob[...].reshape(HC, C)
    for p in (0, 1):
        rows = slice(p * A, (p + 1) * A)
        dagg = contract(dout[rows, :], womat, 1, 1) * dsl[rows, :]
        for b in range(BASIS):
            rr[b * A : (b + 1) * A, :] = (dagg * radial[b : b + 1, mine_c]).astype(BF16)
        part = jnp.dot(mtc[p], rr[...], preferred_element_type=F32)
        if p == 0:
            spread[0:W, :] = part
            rim_s[0] = part[:H].astype(BF16)
        else:
            spread[A:W, :] = spread[A:W, :] + part[: W - A]
            spread[W:, :] = part[W - A :]
            rim_s[1] = part[W - H :].astype(BF16)

    def rim_dn():
        return pltpu.make_async_remote_copy(
            src_ref=rim_s.at[0], dst_ref=rim_hi, send_sem=s_misc.at[6], recv_sem=r_misc.at[6],
            device_id=chip(qp, c), device_id_type=MESH,
        )

    def rim_up():
        return pltpu.make_async_remote_copy(
            src_ref=rim_s.at[1], dst_ref=rim_lo, send_sem=s_misc.at[7], recv_sem=r_misc.at[7],
            device_id=chip(qn, c), device_id_type=MESH,
        )

    @pl.when(q > 0)
    def _():
        rim_dn().start()

    @pl.when(q < 15)
    def _():
        rim_up().start()

    arrived(xo.at[0], s_xo.at[0], r_xo.at[0], left)
    so[4] = (ko[0] + xo[0].astype(F32)).astype(BF16)
    sent.append(send(so.at[4], xo.at[4], s_xo.at[4], r_xo.at[4], right))
    arrived(xo.at[1], s_xo.at[1], r_xo.at[1], right)
    so[5] = (ko[1] + xo[1].astype(F32)).astype(BF16)
    sent.append(send(so.at[5], xo.at[5], s_xo.at[5], r_xo.at[5], left))

    @pl.when(q > 0)
    def _():
        arrived(rim_lo, s_misc.at[7], r_misc.at[7], chip(qp, c))

    @pl.when(q < 15)
    def _():
        arrived(rim_hi, s_misc.at[6], r_misc.at[6], chip(qn, c))

    spread[H : 2 * H, :] = spread[H : 2 * H, :] + rim_lo[...].astype(F32)
    spread[2 * A : 2 * A + H, :] = spread[2 * A : 2 * A + H, :] + rim_hi[...].astype(F32)

    def turned(rows, back, blocks):
        which = jnp.full((rows, FRAG), frag[0], jnp.int32)
        res = []
        for k in range(4):
            v_ = blocks(k)
            for o in range(1, 4):
                hit = jnp.logical_or(which == o, which == o + 4)
                v_ = jnp.where(hit, blocks((k - o if back else k + o) % 4), v_)
            res.append(v_)
        return res

    for k, v in enumerate(
        turned(2 * A, False, lambda k: spread[H : H + 2 * A, k * FRAG : (k + 1) * FRAG])
    ):
        dproj[:, k * FRAG : (k + 1) * FRAG] = v.astype(BF16)

    def msg_part(xd, store_lo, store_hi):
        v_ = jnp.dot(
            feats_t[:, pl.ds(xd, 1)].reshape(2 * A, 2 * A), dproj[...], preferred_element_type=F32
        )
        for k in range(4):
            store_lo(k, v_[:A, k * FRAG : (k + 1) * FRAG])
            store_hi(k, v_[A:, k * FRAG : (k + 1) * FRAG])

    def staged(i):
        def f_(k, v_):
            sm[k, i] = v_.astype(BF16)
        return f_

    def kept(i):
        def f_(k, v_):
            km[k, i] = v_
        return f_

    msg_part(x2, staged(0), staged(1))
    msg_part(xp, kept(0), staged(2))
    msg_part(xn, staged(3), kept(1))
    msg_part(x, kept(2), kept(3))

    def msg_leg(k, i):
        to = (right, left, right, left, right, left)[i]
        send(sm.at[k, i], xm.at[k, i], s_xm.at[0], r_xm.at[k, 0 if i < 2 else 1], to)

    def msg_first(k):
        for i in range(4):
            msg_leg(k, i)

    def msg_relay(k):
        both(xm.at[k, pl.ds(0, 2)], s_xm.at[0], r_xm.at[k, 0]).wait_recv()
        for i in (0, 1):
            sm[k, 4 + i] = (km[k, i] + xm[k, i].astype(F32)).astype(BF16)
            msg_leg(k, 4 + i)

    def msg_y(k):
        both(xm.at[k, pl.ds(2, 4)], s_xm.at[0], r_xm.at[k, 1]).wait_recv()
        lo = (km[k, 2] + xm[k, 3].astype(F32) + xm[k, 4].astype(F32)).astype(BF16)
        hi = (km[k, 3] + xm[k, 2].astype(F32) + xm[k, 5].astype(F32)).astype(BF16)
        sym[k, 0:2] = lo.reshape(2, 2, 32, FRAG)
        sym[k, 2:4] = hi.reshape(2, 2, 32, FRAG)
        for d in (5, 4, 7, 6, 3, 2, 1):
            hh, c_ = (h + d // 2) % 4, (c + d) % 2
            send(
                sym.at[k, hh, c_], ym.at[k, 2 * h + c], s_ym.at[k], r_ym.at[k],
                dev(ylo, hh, x, c_),
            )
        ym[k, 2 * h + c] = sym[k, h, c]

    def msg_sum(k):
        both(ym.at[k, pl.ds(0, 7)], s_ym.at[k], r_ym.at[k]).wait_recv()
        for c_ in (0, 1):
            gm[c_, k] = (
                ym[k, c_].astype(F32) + ym[k, 2 + c_].astype(F32)
                + ym[k, 4 + c_].astype(F32) + ym[k, 6 + c_].astype(F32)
            )

    msg_first(0)
    msg_first(1)

    arrived(xo.at[3], s_xo.at[3], r_xo.at[3], right)
    arrived(xo.at[4], s_xo.at[4], r_xo.at[4], left)
    arrived(xo.at[2], s_xo.at[2], r_xo.at[2], left)
    arrived(xo.at[5], s_xo.at[5], r_xo.at[5], right)
    syo[0] = (ko[2] + xo[3].astype(F32) + xo[4].astype(F32)).astype(BF16).reshape(2, 32, C)
    syo[1] = (ko[3] + xo[2].astype(F32) + xo[5].astype(F32)).astype(BF16).reshape(2, 32, C)

    def yo_copy(e, c_):
        return pltpu.make_async_remote_copy(
            src_ref=syo.at[e, c_], dst_ref=yo.at[h],
            send_sem=s_yo.at[2 * e + c_], recv_sem=r_yo.at[h],
            device_id=dev(ylo, 2 * c + e, x, c_), device_id_type=MESH,
        )

    for e in (0, 1):
        for c_ in (0, 1):
            is_me = jnp.logical_and(2 * c + e == h, c == c_)

            @pl.when(jnp.logical_not(is_me))
            def _(e=e, c_=c_):
                yo_copy(e, c_).start()

            @pl.when(is_me)
            def _(e=e, c_=c_):
                cp = pltpu.make_async_copy(syo.at[e, c_], yo.at[h], loc.at[7])
                cp.start()
                cp.wait()

    msg_relay(0)
    msg_first(2)
    womat = wob[...].reshape(HC, C)
    a_other = act[pl.ds(pl.multiple_of((1 - c) * A, A), A), :]
    part_s[...] = jnp.dot(a_other, womat, preferred_element_type=F32).astype(BF16)
    sent.append(send(part_s, part_r, s_misc.at[8], r_misc.at[8], partner))
    a_own = act[pl.ds(pl.multiple_of(c * A, A), A), :]
    node_own = jnp.dot(a_own, womat, preferred_element_type=F32) + fx[f_rows, :].astype(F32)
    msg_relay(1)
    msg_first(3)
    msg_relay(2)
    msg_y(0)
    msg_relay(3)
    msg_y(1)
    for h_ in range(4):
        @pl.when(jnp.logical_or(h_ != h, c != half))
        def _(h_=h_):
            arrived(yo.at[h_], s_yo.at[0], r_yo.at[h_], dev(ylo, h_, x, half))

    total = yo[0].astype(F32) + yo[1].astype(F32) + yo[2].astype(F32) + yo[3].astype(F32)
    gout_o[0] = total.astype(BF16)
    put(2, gout_o, gout_h)
    gf[...] = total
    chosen = jnp.full((32, FRAG), frag[0], jnp.int32)

    def decoded(piece):
        scale = (jnp.max(jnp.abs(piece), axis=1, keepdims=True) + TINY).astype(BF16).astype(F32)
        code = (piece / scale).astype(BF16).astype(F32)
        return (scale * code).astype(BF16)

    peers = sorted(
        ((dy, dz) for dy in range(2) for dz in range(8) if dy or dz),
        key=lambda p_: -(p_[0] + min(p_[1], 8 - p_[1])),
    )

    def outer_send(m, buf, ss, rs):
        for dy, dz in peers:
            to = ((ylo + dy) % 2 * 8 + (z + dz) % 8, f)
            send(tb.at[m], buf.at[r], ss.at[0], rs.at[0], to)

    def outer_sum(m, buf, ss, rs):
        both(buf.at[pl.ds(0, 15)], ss.at[0], rs.at[0]).wait_recv()
        outer_o[m] = jnp.sum(buf[...].astype(F32), axis=0)

    piece = jnp.zeros((32, FRAG), F32)
    for b in range(C // FRAG):
        piece = jnp.where(chosen == b, gf[:, b * FRAG : (b + 1) * FRAG], piece)
    term = decoded(piece)
    tb[1] = term
    oo[r] = term
    outer_send(1, oo, s_oo, r_oo)

    msg_y(2)
    msg_y(3)
    msg_sum(0)
    term = decoded(jnp.where(chosen < 4, gm[0, 0], gm[1, 0]))
    tb[0] = term
    om[r] = term
    outer_send(0, om, s_om, r_om)
    arrived(part_r, s_misc.at[8], r_misc.at[8], partner)
    node_o[...] = (node_own + part_r[...].astype(F32)).astype(BF16)
    put(0, node_o, node_h)
    outer_sum(1, oo, s_oo, r_oo)
    for k in (1, 2, 3):
        msg_sum(k)
    for c_ in (0, 1):
        for k, v in enumerate(turned(32, True, lambda k: gm[c_, k])):
            gmsg_o[0, :, c_ * HC + k * FRAG : c_ * HC + (k + 1) * FRAG] = v.astype(BF16)
    put(1, gmsg_o, gmsg_h)
    outer_sum(0, om, s_om, r_om)
    put(3, outer_o, outer_h)

    for cp in puts:
        cp.wait()
    both(sm, s_xm.at[0], s_xm.at[0]).wait_send()
    both(idb.at[pl.ds(0, 3)], s_ix.at[0], r_ix.at[0]).wait_send()
    for k in range(4):
        both(ym.at[k, pl.ds(0, 7)], s_ym.at[k], r_ym.at[k]).wait_send()
    both(oo.at[pl.ds(0, 15)], s_oo.at[0], r_oo.at[0]).wait_send()
    both(om.at[pl.ds(0, 15)], s_om.at[0], r_om.at[0]).wait_send()
    for cp in sent:
        cp.wait_send()

    @pl.when(up_ok)
    def _():
        for c_ in (0, 1):
            up_copy(c_).wait_send()

    @pl.when(dn_ok)
    def _():
        for c_ in (0, 1):
            dn_copy(c_).wait_send()

    @pl.when(half != c)
    def _():
        wo_partner().wait_send()

    for n in (0, 1):
        both(wmb.at[0, pl.ds(0, 3)], s_wx.at[n], s_wx.at[n]).wait_send()
    both(wmb.at[0], s_wz.at[1], r_wz.at[1]).wait_send()

    for parity in (0, 1):
        @pl.when(par == parity)
        def _(parity=parity):
            for j in y_of[parity]:
                for c_ in (0, 1):
                    wm_y(j, c_).wait_send()
            ref = wmb.at[0] if parity else wmb.at[0, pl.ds(0, 3)]
            both(ref, s_wz.at[0], r_wz.at[0]).wait_send()

    @pl.when(h % 2 == par)
    def _():
        for j in range(3):
            wo_y(j).wait_send()

    @pl.when(h != 2 * c + par)
    def _():
        both(wob.at[0], s_oz.at[0], r_oz.at[0]).wait_send()

    @pl.when(h == 2 * c + par)
    def _():
        both(wob.at[0, pl.ds(0, 3)], s_oz.at[0], r_oz.at[0]).wait_send()
    @pl.when(q > 0)
    def _():
        rim_dn().wait_send()

    @pl.when(q < 15)
    def _():
        rim_up().wait_send()

    for e in (0, 1):
        for c_ in (0, 1):
            @pl.when(jnp.logical_not(jnp.logical_and(2 * c + e == h, c == c_)))
            def _(e=e, c_=c_):
                yo_copy(e, c_).wait_send()


def finish(*refs):
    sems = refs[8]
    copies = [pltpu.make_async_copy(refs[i], refs[4 + i], sems.at[i]) for i in range(4)]
    for cp in copies:
        cp.start()
    for cp in copies:
        cp.wait()


def shards(feats, src, dist, ids, wm, wo, radial, cot, frag):
    vm = pl.BlockSpec(memory_space=pltpu.VMEM)
    dma = lambda *n: pltpu.SemaphoreType.DMA(n)
    V = pltpu.VMEM
    results = pl.pallas_call(
        body,
        out_shape=(
            jax.ShapeDtypeStruct((A, C), BF16),
            jax.ShapeDtypeStruct((1, 32, C), BF16),
            jax.ShapeDtypeStruct((1, 32, C), BF16),
            jax.ShapeDtypeStruct((2, 32, FRAG), F32),
        ),
        in_specs=[pl.BlockSpec(memory_space=pl.ANY)] * 8 + [pl.BlockSpec(memory_space=pltpu.SMEM)],
        out_specs=(pl.BlockSpec(memory_space=pl.ANY),) * 4,
        scratch_shapes=[
            V((4, 4, 2, 32, HC), BF16),
            V((2, 4, 2, 32, C), BF16),
            V((32, C), BF16),
            V((32, C), BF16),
            V((BASIS, C), F32),
            V((4, 4, 2, 1, A), jnp.int32),
            V((EXT, C), BF16),
            V((2, A, C), BF16),
            V((2, NB, A), jnp.int32),
            V((2, NB, A), F32),
            V((A, C), BF16),
            V((H, HC), BF16),
            V((H, HC), BF16),
            V((6, 64, C), BF16),
            V((4, 6, A, FRAG), BF16),
            V((4, 32, C), BF16),
            V((4, 8, 32, FRAG), BF16),
            V((16, 32, FRAG), BF16),
            V((16, 32, FRAG), BF16),
            V((BASIS, NB, A), F32),
            V((BASIS * W, A), F32),
            V((2, W, BASIS * A), BF16),
            V((2, A, BASIS * W), BF16),
            V((BASIS * W, HC), BF16),
            V((2 * A, HC), BF16),
            V((2 * A, HC), F32),
            V((2, 4, 64, 2 * A), BF16),
            V((4, 4, 64, 2 * A), BF16),
            V((2 * A, C), BF16),
            V((BASIS * A, HC), BF16),
            V((EXT, HC), F32),
            V((2 * A, HC), BF16),
            V((A, C), BF16),
            V((2, H, HC), BF16),
            V((6, 64, C), BF16),
            V((4, 64, C), F32),
            V((4, 6, A, FRAG), BF16),
            V((4, 4, A, FRAG), F32),
            V((2, 2, 32, C), BF16),
            V((4, 4, 2, 32, FRAG), BF16),
            V((32, C), F32),
            V((2, 4, 32, FRAG), F32),
            V((2, 32, FRAG), BF16),
            V((A, C), BF16),
            V((1, 32, C), BF16),
            V((1, 32, C), BF16),
            V((2, 32, FRAG), F32),
            dma(14),
            dma(7), dma(7), dma(7), dma(7), dma(4), dma(7),
            dma(2), dma(2, 3), dma(2), dma(2), dma(1), dma(1),
            dma(4), dma(4), dma(1), dma(1),
            dma(9), dma(9), dma(6), dma(6), dma(1), dma(4, 2),
            dma(4), dma(4), dma(4), dma(4), dma(1), dma(1), dma(1), dma(1),
        ],
        compiler_params=pltpu.CompilerParams(
            collective_id=0, has_side_effects=True, vmem_limit_bytes=56 << 20
        ),
        name="step",
    )(feats, src, dist, ids, wm, wo, radial, cot, frag)
    anywhere = pl.BlockSpec(memory_space=pl.ANY)
    return pl.pallas_call(
        finish,
        out_shape=tuple(jax.ShapeDtypeStruct(v.shape, v.dtype) for v in results),
        in_specs=[vm] * 4,
        out_specs=(anywhere,) * 4,
        scratch_shapes=[dma(4)],
        compiler_params=pltpu.CompilerParams(vmem_limit_bytes=60 << 20),
        name="finish",
    )(*results)


def solution(mesh):
    placed = (
        P(("replica", "fsdp"), None),
        P(None, ("replica", "fsdp")),
        P(None, ("replica", "fsdp")),
        P("replica", "fsdp"),
        P("fsdp", None),
        P("fsdp", None),
        P(),
        P(("replica", "fsdp"), None),
        P(),
    )
    return jax.shard_map(
        shards,
        mesh=mesh,
        in_specs=placed,
        out_specs=(
            P(("replica", "fsdp"), None),
            P("replica", "fsdp", None),
            P("replica", "fsdp", None),
            P(None, "fsdp", None),
        ),
        check_vma=False,
    )
```

```python
import functools
import math

import jax
import jax.numpy as jnp
from jax import lax
from jax.experimental import pallas as pl
from jax.experimental.pallas import tpu as pltpu
from jax.sharding import PartitionSpec as P

MESH = pl.DeviceIdType.MESH
F32 = jnp.float32
BF16 = jnp.bfloat16
GRAPHS = 8
FRAG = 128
A = 128
C = 1024
HC = 512
H = 32
NB = 12
BASIS = 8
W = 2 * A - 64
EXT = 2 * A + 2 * H
TINY = 1e-6


def contract(a, b, da, db):
    return lax.dot_general(a, b, (((da,), (db,)), ((), ())), preferred_element_type=F32)


def body(
    feats, src, dist, ids, wm, wo, radial_h, cot, frag,
    node_h, gmsg_h, gout_h, outer_h,
    wmb, wob, wmv, wov, radial, idb, fx, cotb, srcb, distb, part_r,
    rim_lo, rim_hi, xo, xm, yo, ym, oo, om,
    bas, mtv, mtc, mc, ps, act, dsl, act_t, feats_t, dout, rr, spread, dproj,
    part_s, rim_s, so, ko, sm, km, syo, sym, gf, gm, tb, node_o, gmsg_o, gout_o, outer_o,
    loc, s_wy, r_wy, s_iy, r_iy, s_oy, r_oy, s_wx, r_wx, s_wz, r_wz, s_ix, r_ix,
    s_ox, r_ox, s_oz, r_oz,
    s_misc, r_misc, s_xo, r_xo, s_xm, r_xm, s_yo, r_yo, s_ym, r_ym, s_oo, r_oo, s_om, r_om,
):
    r = lax.axis_index("replica")
    f = lax.axis_index("fsdp")
    ylo, z = r // 8, r % 8
    h, x, c = f // 8, (f // 2) % 4, f % 2
    q = f // 2
    s = 2 * ylo - 1
    xp, xn, x2 = (x + 1) % 4, (x + 3) % 4, (x + 2) % 4
    ha, hb, h2 = (h + s + 4) % 4, (h - s + 4) % 4, (h + 2) % 4
    half = h // 2
    par = z % 2

    def dev(ylo_, h_, x_, c_):
        return (ylo_ * 8 + z, h_ * 8 + x_ * 2 + c_)

    def chip(q_, c_):
        return (r, q_ * 2 + c_)

    partner = dev(ylo, h, x, 1 - c)
    right, left = dev(ylo, h, xp, c), dev(ylo, h, xn, c)
    qn, qp = (q + 1) % 16, (q + 15) % 16
    y_to = ((1 - ylo, ha), (ylo, ha), (1 - ylo, h2))
    y_in = (ha, hb, h2)
    y_from = ((1 - ylo, ha), (ylo, hb), (1 - ylo, h2))

    def send(a_, b_, ss, rs, to):
        cp = pltpu.make_async_remote_copy(
            src_ref=a_, dst_ref=b_, send_sem=ss, recv_sem=rs, device_id=to, device_id_type=MESH
        )
        cp.start()
        return cp

    def arrived(b_, ss, rs, frm):
        pltpu.make_async_remote_copy(
            src_ref=b_, dst_ref=b_, send_sem=ss, recv_sem=rs, device_id=frm, device_id_type=MESH
        ).wait_recv()

    def put(i, a_, b_):
        cp = pltpu.make_async_copy(a_, b_, loc.at[10 + i])
        cp.start()
        puts.append(cp)

    puts = []
    def both(ref, ss, rs):
        return pltpu.make_async_remote_copy(
            src_ref=ref, dst_ref=ref, send_sem=ss, recv_sem=rs, device_id=partner,
            device_id_type=MESH,
        )

    bar = pltpu.get_barrier_semaphore()
    greet = [partner]
    for c_ in (0, 1):
        greet += [dev(ylo, h, x_, c_) for x_ in (xp, xn, x2)]
        greet += [
            dev(ylo, ha, x, c_), dev(ylo, hb, x, c_), dev(ylo, h2, x, c_),
            dev(1 - ylo, ha, x, c_), dev(1 - ylo, h2, x, c_), chip(qn, c_), chip(qp, c_),
        ]
    greet += [((r + d) % 16, f) for d in range(1, 16)]
    for g in greet:
        pl.semaphore_signal(bar, inc=1, device_id=g, device_id_type=MESH)

    f_rows = pl.ds(pl.multiple_of(H + A * c, H), A)
    f_other = pl.ds(pl.multiple_of(H + A * (1 - c), H), A)
    own = [
        pltpu.make_async_copy(a_, b_, loc.at[i])
        for i, (a_, b_) in enumerate(
            (
                (wm, wmv),
                (wm.at[:, pl.ds(pl.multiple_of(c * HC, HC), HC)], wmb.at[h, x, c]),
                (ids, idb.at[h, x, c]),
                (src, srcb.at[c]),
                (dist, distb.at[c]),
                (feats, fx.at[f_rows]),
                (wo, wov),
                (cot, cotb.at[c]),
                (radial_h, radial),
            )
        )
    ]
    for o in own:
        o.start()

    @pl.when(half == c)
    def _():
        cp = pltpu.make_async_copy(wo, wob.at[h % 2, x, c], loc.at[9])
        cp.start()
        cp.wait()

    @pl.when(q == 0)
    def _():
        fx[0:H, :] = jnp.zeros((H, C), BF16)
        rim_lo[...] = jnp.zeros((H, HC), BF16)

    @pl.when(q == 15)
    def _():
        fx[H + 2 * A :, :] = jnp.zeros((H, C), BF16)
        rim_hi[...] = jnp.zeros((H, HC), BF16)

    for o in own:
        o.wait()
    pl.semaphore_wait(bar, len(greet))

    sent = []
    other = pl.ds(pl.multiple_of((1 - c) * HC, HC), HC)
    mine_c = pl.ds(pl.multiple_of(c * HC, HC), HC)
    my_ids = idb.at[h, x, c]
    sent.append(send(my_ids, my_ids, s_iy.at[6], r_iy.at[6], partner))
    for j, hh in enumerate((hb, ha, h2)):
        for c_ in (0, 1):
            sent.append(
                send(
                    my_ids, my_ids, s_iy.at[2 * j + c_], r_iy.at[2 * j + c], dev(ylo, hh, x, c_)
                )
            )
    sent.append(send(wmv.at[:, other], wmb.at[h, x, c], s_wy.at[6], r_wy.at[6], partner))

    def wm_y(j, c_):
        yl, hh = y_to[j]
        return pltpu.make_async_remote_copy(
            src_ref=wmv.at[:, pl.ds(c_ * HC, HC)], dst_ref=wmb.at[h, x, c],
            send_sem=s_wy.at[2 * j + c_], recv_sem=r_wy.at[2 * j + c],
            device_id=dev(yl, hh, x, c_), device_id_type=MESH,
        )

    def wo_y(j):
        yl, hh = y_to[j]
        return pltpu.make_async_remote_copy(
            src_ref=wov, dst_ref=wob.at[h % 2, x, c],
            send_sem=s_oy.at[j], recv_sem=r_oy.at[2 * j + c],
            device_id=dev(yl, hh, x, half), device_id_type=MESH,
        )

    y_of = ((2,), (0, 1))
    for parity in (0, 1):
        @pl.when(par == parity)
        def _(parity=parity):
            for j in y_of[parity]:
                for c_ in (0, 1):
                    wm_y(j, c_).start()

    @pl.when(h % 2 == par)
    def _():
        for j in (2, 1, 0):
            wo_y(j).start()

    sent.append(send(srcb.at[c], srcb.at[c], s_misc.at[0], r_misc.at[0], partner))
    sent.append(send(distb.at[c], distb.at[c], s_misc.at[1], r_misc.at[1], partner))
    def wm_in(k):
        if k == 0:
            arrived(wmb.at[h, x, 1 - c], s_wy.at[6], r_wy.at[6], partner)
        else:
            for c_ in (0, 1):
                i = 2 * (k - 1) + c_
                arrived(
                    wmb.at[y_in[k - 1], x, c_], s_wy.at[i], r_wy.at[i], dev(*y_from[k - 1], x, c_)
                )

    taken = ((h + par * s + 4) % 4, (h + 2 * (1 - par) - par * s + 4) % 4)
    rest = ((h + (1 - par) * s + 4) % 4, (h + 2 * par - (1 - par) * s + 4) % 4)
    z_to = ((ylo * 8 + (z + 1) % 8, f), (ylo * 8 + (z + 7) % 8, f))
    z_in = (z_to[1], z_to[0])

    far = dev(ylo, h, x2, c)

    def wm_x(n, i):
        ref = wmb.at[taken[n], x]
        return pltpu.make_async_remote_copy(
            src_ref=ref, dst_ref=ref, send_sem=s_wx.at[n], recv_sem=r_wx.at[n, i],
            device_id=(right, left, far)[i], device_id_type=MESH,
        )

    def wm_z(n, i, u):
        ref = wmb.at[taken[n], (xn, xp, x2, x)[i], u]
        return pltpu.make_async_remote_copy(
            src_ref=ref, dst_ref=ref, send_sem=s_wz.at[n], recv_sem=r_wz.at[n],
            device_id=z_to[u], device_id_type=MESH,
        )

    def wm_x_start(n, parity):
        @pl.when(par == parity)
        def _():
            if n or parity:
                wm_in(3 if parity == 0 else 1 + n)
            for i in range(3):
                wm_x(n, i).start()
            if n or parity:
                for u in (0, 1):
                    wm_z(n, 3, u).start()

    def wm_x_in(n, i):
        ref = wmb.at[taken[n], (xn, xp, x2)[i]]
        arrived(ref, s_wx.at[n], r_wx.at[n, i], (left, right, far)[i])
        for u in (0, 1):
            wm_z(n, i, u).start()

    norm = 1.0 / math.sqrt(NB)
    PARTS = 2

    def build(p, part):
        if part == 0:
            d = distb[p]
            env = 0.5 * (jnp.cos(d * (math.pi / 5.0)) + 1.0) * norm
            for b in range(BASIS):
                bas[b] = jnp.exp(-2.0 * (d - 5.0 * b / (BASIS - 1)) ** 2) * env
        base = 2 * A * q - H + A * p

        def tile(t, carry):
            row = pl.multiple_of(t * 16, 16)
            at = row + base + lax.broadcasted_iota(jnp.int32, (16, A), 0)
            accs = [jnp.zeros((16, A), F32) for _ in range(BASIS)]
            for k in range(NB):
                hit = srcb[p, k : k + 1, :] == at
                for b in range(BASIS):
                    accs[b] = accs[b] + jnp.where(hit, bas[b, k : k + 1, :], 0.0)
            for b in range(BASIS):
                mtv[pl.ds(pl.multiple_of(b * W + row, 16), 16), :] = accs[b]
                mtc[p, pl.ds(row, 16), b * A : (b + 1) * A] = accs[b].astype(BF16)
            return carry

        step = W // 16 // PARTS
        lax.fori_loop(part * step, (part + 1) * step, tile, 0)
        if part == PARTS - 1:
            for t in range(BASIS * W // A):
                mc[p, :, t * A : (t + 1) * A] = mtv[t * A : (t + 1) * A, :].T.astype(BF16)

    wm_in(0)
    wm_x_start(0, 0)

    def wo_partner():
        return pltpu.make_async_remote_copy(
            src_ref=wov, dst_ref=wob.at[h % 2, x, c], send_sem=s_oy.at[3], recv_sem=r_oy.at[6],
            device_id=partner, device_id_type=MESH,
        )

    @pl.when(half != c)
    def _():
        wo_partner().start()

    up_ok = jnp.logical_and(c == 1, q < 15)
    dn_ok = jnp.logical_and(c == 0, q > 0)

    def up_copy(c_):
        return pltpu.make_async_remote_copy(
            src_ref=fx.at[pl.ds(2 * A, H)], dst_ref=fx.at[pl.ds(0, H)],
            send_sem=s_misc.at[4 + c_], recv_sem=r_misc.at[4],
            device_id=chip(qn, c_), device_id_type=MESH,
        )

    def dn_copy(c_):
        return pltpu.make_async_remote_copy(
            src_ref=fx.at[pl.ds(H, H)], dst_ref=fx.at[pl.ds(H + 2 * A, H)],
            send_sem=s_misc.at[4 + c_], recv_sem=r_misc.at[5],
            device_id=chip(qp, c_), device_id_type=MESH,
        )

    @pl.when(up_ok)
    def _():
        for c_ in (0, 1):
            up_copy(c_).start()

    @pl.when(dn_ok)
    def _():
        for c_ in (0, 1):
            dn_copy(c_).start()

    sent.append(send(fx.at[f_rows], fx.at[f_rows], s_misc.at[2], r_misc.at[2], partner))
    sent.append(send(cotb.at[c], cotb.at[c], s_misc.at[3], r_misc.at[3], partner))

    def wo_in():
        @pl.when(h == 2 * c + par)
        def _():
            arrived(wob.at[par, x, 1 - c], s_oy.at[3], r_oy.at[6], partner)

        for j in range(3):
            @pl.when(y_in[j] == 2 * c + par)
            def _(j=j):
                for c_ in (0, 1):
                    arrived(
                        wob.at[par, x, c_], s_oy.at[0], r_oy.at[2 * j + c_],
                        dev(*y_from[j], x, c_),
                    )

        for i, to in enumerate((right, left, far)):
            ref = wob.at[par, x]
            sent.append(send(ref, ref, s_ox.at[i], r_ox.at[i], to))

    def wo_own_z(u):
        ref = wob.at[par, x, u]
        return pltpu.make_async_remote_copy(
            src_ref=ref, dst_ref=ref, send_sem=s_oz.at[0], recv_sem=r_oz.at[0],
            device_id=z_to[u], device_id_type=MESH,
        )

    def wo_z():
        @pl.when(h != 2 * c + par)
        def _():
            for u in (0, 1):
                wo_own_z(u).start()

    def wo_x_in(i):
        col = (xn, xp, x2)[i]
        arrived(wob.at[par, col], s_ox.at[i], r_ox.at[i], (left, right, far)[i])
        for u in (0, 1):
            ref = wob.at[par, col, u]
            send(ref, ref, s_oz.at[0], r_oz.at[0], z_to[u])

    arrived(srcb.at[1 - c], s_misc.at[0], r_misc.at[0], partner)
    arrived(distb.at[1 - c], s_misc.at[1], r_misc.at[1], partner)
    build(0, 0)
    wm_x_start(0, 1)
    wm_x_start(1, 0)
    wm_x_start(1, 1)
    build(0, 1)
    arrived(idb.at[h, x, 1 - c], s_iy.at[6], r_iy.at[6], partner)
    for k, yb in enumerate(y_in):
        for c_ in (0, 1):
            i = 2 * k + c_
            arrived(idb.at[yb, x, c_], s_iy.at[i], r_iy.at[i], dev(ylo, yb, x, c_))
    for i, x_ in enumerate((xp, xn, x2)):
        ref = idb.at[:, x]
        send(ref, ref, s_ix.at[0], r_ix.at[0], dev(ylo, h, x_, c))
    wm_x_in(0, 0)
    wm_x_in(0, 1)
    wo_in()
    build(1, 0)
    wm_x_in(0, 2)
    wm_x_in(1, 1)
    wm_x_in(1, 0)
    wm_x_in(1, 2)
    wo_z()
    build(1, 1)
    arrived(fx.at[f_other], s_misc.at[2], r_misc.at[2], partner)
    for p in (0, 1):
        feats_t[:, :, :, p * A : (p + 1) * A] = (
            fx[H + p * A : H + (p + 1) * A, :].T.reshape(4, 4, 64, A)
        )
    arrived(cotb.at[1 - c], s_misc.at[3], r_misc.at[3], partner)

    @pl.when(q > 0)
    def _():
        arrived(fx.at[pl.ds(0, H)], s_misc.at[4], r_misc.at[4], chip(qp, 1))

    @pl.when(q < 15)
    def _():
        arrived(fx.at[pl.ds(H + 2 * A, H)], s_misc.at[4], r_misc.at[5], chip(qn, 0))

    both(idb.at[pl.ds(0, 3)], s_ix.at[0], r_ix.at[0]).wait_recv()
    all_ids = idb[...].reshape(32, A)
    for p in (0, 1):
        mine = idb[h, x, p]
        wrow = jnp.zeros((1, A), F32)
        for g in range(GRAPHS):
            count = jnp.sum((all_ids == g).astype(F32), axis=0, keepdims=True)
            count = jnp.sum(count, axis=1, keepdims=True)
            wrow = wrow + jnp.where(mine == g, lax.rsqrt(jnp.broadcast_to(count, (1, A))), 0.0)
        wcol = jnp.broadcast_to(wrow, (A, A)).T
        for t in range(C // A):
            cols = slice(t * A, (t + 1) * A)
            dout[p * A : (p + 1) * A, cols] = (cotb[p, :, cols].astype(F32) * wcol).astype(BF16)

    wo_x_in(0)
    wo_x_in(1)
    both(wmb.at[0], s_wz.at[1], r_wz.at[1]).wait_recv()
    for parity in (0, 1):
        @pl.when(par == parity)
        def _(parity=parity):
            ref = wmb.at[0, pl.ds(0, 3)] if parity else wmb.at[0]
            both(ref, s_wz.at[0], r_wz.at[0]).wait_recv()

    wmat = wmb[...].reshape(C, HC)
    proj = jnp.dot(fx[...], wmat, preferred_element_type=F32).astype(BF16)
    spread[...] = proj.astype(F32)
    for p in (0, 1):
        for b in range(BASIS):
            ps[b * W : (b + 1) * W, :] = (
                spread[p * A : p * A + W, :] * radial[b : b + 1, mine_c]
            ).astype(BF16)
        agg = jnp.dot(mc[p], ps[...], preferred_element_type=F32)
        sig = 1.0 / (1.0 + jnp.exp(-agg))
        a16 = (agg * sig).astype(BF16)
        rows = slice(p * A, (p + 1) * A)
        act[rows, :] = a16
        dsl[rows, :] = sig * (1.0 + agg * (1.0 - sig))
        act_t[:, :, :, rows] = a16.T.reshape(2, 4, 64, A)

    wo_x_in(2)
    def out_part(xd):
        return jnp.dot(
            act_t[:, pl.ds(xd, 1)].reshape(A, 2 * A), dout[...], preferred_element_type=F32
        )

    v = out_part(x2)
    so[0] = v[:64].astype(BF16)
    so[1] = v[64:].astype(BF16)
    sent.append(send(so.at[0], xo.at[0], s_xo.at[0], r_xo.at[0], right))
    sent.append(send(so.at[1], xo.at[1], s_xo.at[1], r_xo.at[1], left))
    v = out_part(xp)
    ko[0] = v[:64]
    so[2] = v[64:].astype(BF16)
    sent.append(send(so.at[2], xo.at[2], s_xo.at[2], r_xo.at[2], right))
    v = out_part(xn)
    so[3] = v[:64].astype(BF16)
    ko[1] = v[64:]
    sent.append(send(so.at[3], xo.at[3], s_xo.at[3], r_xo.at[3], left))
    v = out_part(x)
    ko[2] = v[:64]
    ko[3] = v[64:]

    @pl.when(h != 2 * c + 1 - par)
    def _():
        both(wob.at[0], s_oz.at[0], r_oz.at[0]).wait_recv()

    @pl.when(h == 2 * c + 1 - par)
    def _():
        both(wob.at[0, pl.ds(0, 3)], s_oz.at[0], r_oz.at[0]).wait_recv()

    @pl.when(h == 2 * c + 1 - par)
    def _():
        arrived(wob.at[1 - par, x, 1 - c], s_oy.at[3], r_oy.at[6], partner)

    womat = wob[...].reshape(HC, C)
    for p in (0, 1):
        rows = slice(p * A, (p + 1) * A)
        dagg = contract(dout[rows, :], womat, 1, 1) * dsl[rows, :]
        for b in range(BASIS):
            rr[b * A : (b + 1) * A, :] = (dagg * radial[b : b + 1, mine_c]).astype(BF16)
        part = jnp.dot(mtc[p], rr[...], preferred_element_type=F32)
        if p == 0:
            spread[0:W, :] = part
            rim_s[0] = part[:H].astype(BF16)
        else:
            spread[A:W, :] = spread[A:W, :] + part[: W - A]
            spread[W:, :] = part[W - A :]
            rim_s[1] = part[W - H :].astype(BF16)

    def rim_dn():
        return pltpu.make_async_remote_copy(
            src_ref=rim_s.at[0], dst_ref=rim_hi, send_sem=s_misc.at[6], recv_sem=r_misc.at[6],
            device_id=chip(qp, c), device_id_type=MESH,
        )

    def rim_up():
        return pltpu.make_async_remote_copy(
            src_ref=rim_s.at[1], dst_ref=rim_lo, send_sem=s_misc.at[7], recv_sem=r_misc.at[7],
            device_id=chip(qn, c), device_id_type=MESH,
        )

    @pl.when(q > 0)
    def _():
        rim_dn().start()

    @pl.when(q < 15)
    def _():
        rim_up().start()

    arrived(xo.at[0], s_xo.at[0], r_xo.at[0], left)
    so[4] = (ko[0] + xo[0].astype(F32)).astype(BF16)
    sent.append(send(so.at[4], xo.at[4], s_xo.at[4], r_xo.at[4], right))
    arrived(xo.at[1], s_xo.at[1], r_xo.at[1], right)
    so[5] = (ko[1] + xo[1].astype(F32)).astype(BF16)
    sent.append(send(so.at[5], xo.at[5], s_xo.at[5], r_xo.at[5], left))

    @pl.when(q > 0)
    def _():
        arrived(rim_lo, s_misc.at[7], r_misc.at[7], chip(qp, c))

    @pl.when(q < 15)
    def _():
        arrived(rim_hi, s_misc.at[6], r_misc.at[6], chip(qn, c))

    spread[H : 2 * H, :] = spread[H : 2 * H, :] + rim_lo[...].astype(F32)
    spread[2 * A : 2 * A + H, :] = spread[2 * A : 2 * A + H, :] + rim_hi[...].astype(F32)

    def turned(rows, back, blocks):
        which = jnp.full((rows, FRAG), frag[0], jnp.int32)
        res = []
        for k in range(4):
            v_ = blocks(k)
            for o in range(1, 4):
                hit = jnp.logical_or(which == o, which == o + 4)
                v_ = jnp.where(hit, blocks((k - o if back else k + o) % 4), v_)
            res.append(v_)
        return res

    for k, v in enumerate(
        turned(2 * A, False, lambda k: spread[H : H + 2 * A, k * FRAG : (k + 1) * FRAG])
    ):
        dproj[:, k * FRAG : (k + 1) * FRAG] = v.astype(BF16)

    def msg_part(xd, store_lo, store_hi):
        v_ = jnp.dot(
            feats_t[:, pl.ds(xd, 1)].reshape(2 * A, 2 * A), dproj[...], preferred_element_type=F32
        )
        for k in range(4):
            store_lo(k, v_[:A, k * FRAG : (k + 1) * FRAG])
            store_hi(k, v_[A:, k * FRAG : (k + 1) * FRAG])

    def staged(i):
        def f_(k, v_):
            sm[k, i] = v_.astype(BF16)
        return f_

    def kept(i):
        def f_(k, v_):
            km[k, i] = v_
        return f_

    msg_part(x2, staged(0), staged(1))
    msg_part(xp, kept(0), staged(2))
    msg_part(xn, staged(3), kept(1))
    msg_part(x, kept(2), kept(3))

    def msg_leg(k, i):
        to = (right, left, right, left, right, left)[i]
        send(sm.at[k, i], xm.at[k, i], s_xm.at[0], r_xm.at[k, 0 if i < 2 else 1], to)

    def msg_first(k):
        for i in range(4):
            msg_leg(k, i)

    def msg_relay(k):
        both(xm.at[k, pl.ds(0, 2)], s_xm.at[0], r_xm.at[k, 0]).wait_recv()
        for i in (0, 1):
            sm[k, 4 + i] = (km[k, i] + xm[k, i].astype(F32)).astype(BF16)
            msg_leg(k, 4 + i)

    def msg_y(k):
        both(xm.at[k, pl.ds(2, 4)], s_xm.at[0], r_xm.at[k, 1]).wait_recv()
        lo = (km[k, 2] + xm[k, 3].astype(F32) + xm[k, 4].astype(F32)).astype(BF16)
        hi = (km[k, 3] + xm[k, 2].astype(F32) + xm[k, 5].astype(F32)).astype(BF16)
        sym[k, 0:2] = lo.reshape(2, 2, 32, FRAG)
        sym[k, 2:4] = hi.reshape(2, 2, 32, FRAG)
        for d in (5, 4, 7, 6, 3, 2, 1):
            hh, c_ = (h + d // 2) % 4, (c + d) % 2
            send(
                sym.at[k, hh, c_], ym.at[k, 2 * h + c], s_ym.at[k], r_ym.at[k],
                dev(ylo, hh, x, c_),
            )
        ym[k, 2 * h + c] = sym[k, h, c]

    def msg_sum(k):
        both(ym.at[k, pl.ds(0, 7)], s_ym.at[k], r_ym.at[k]).wait_recv()
        for c_ in (0, 1):
            gm[c_, k] = (
                ym[k, c_].astype(F32) + ym[k, 2 + c_].astype(F32)
                + ym[k, 4 + c_].astype(F32) + ym[k, 6 + c_].astype(F32)
            )

    msg_first(0)
    msg_first(1)

    arrived(xo.at[3], s_xo.at[3], r_xo.at[3], right)
    arrived(xo.at[4], s_xo.at[4], r_xo.at[4], left)
    arrived(xo.at[2], s_xo.at[2], r_xo.at[2], left)
    arrived(xo.at[5], s_xo.at[5], r_xo.at[5], right)
    syo[0] = (ko[2] + xo[3].astype(F32) + xo[4].astype(F32)).astype(BF16).reshape(2, 32, C)
    syo[1] = (ko[3] + xo[2].astype(F32) + xo[5].astype(F32)).astype(BF16).reshape(2, 32, C)

    def yo_copy(e, c_):
        return pltpu.make_async_remote_copy(
            src_ref=syo.at[e, c_], dst_ref=yo.at[h],
            send_sem=s_yo.at[2 * e + c_], recv_sem=r_yo.at[h],
            device_id=dev(ylo, 2 * c + e, x, c_), device_id_type=MESH,
        )

    for e in (0, 1):
        for c_ in (0, 1):
            is_me = jnp.logical_and(2 * c + e == h, c == c_)

            @pl.when(jnp.logical_not(is_me))
            def _(e=e, c_=c_):
                yo_copy(e, c_).start()

            @pl.when(is_me)
            def _(e=e, c_=c_):
                cp = pltpu.make_async_copy(syo.at[e, c_], yo.at[h], loc.at[7])
                cp.start()
                cp.wait()

    msg_relay(0)
    msg_first(2)
    womat = wob[...].reshape(HC, C)
    a_other = act[pl.ds(pl.multiple_of((1 - c) * A, A), A), :]
    part_s[...] = jnp.dot(a_other, womat, preferred_element_type=F32).astype(BF16)
    sent.append(send(part_s, part_r, s_misc.at[8], r_misc.at[8], partner))
    a_own = act[pl.ds(pl.multiple_of(c * A, A), A), :]
    node_own = jnp.dot(a_own, womat, preferred_element_type=F32) + fx[f_rows, :].astype(F32)
    msg_relay(1)
    msg_first(3)
    msg_relay(2)
    msg_y(0)
    msg_relay(3)
    msg_y(1)
    for h_ in range(4):
        @pl.when(jnp.logical_or(h_ != h, c != half))
        def _(h_=h_):
            arrived(yo.at[h_], s_yo.at[0], r_yo.at[h_], dev(ylo, h_, x, half))

    total = yo[0].astype(F32) + yo[1].astype(F32) + yo[2].astype(F32) + yo[3].astype(F32)
    gout_o[0] = total.astype(BF16)
    put(2, gout_o, gout_h)
    gf[...] = total
    chosen = jnp.full((32, FRAG), frag[0], jnp.int32)

    def decoded(piece):
        scale = (jnp.max(jnp.abs(piece), axis=1, keepdims=True) + TINY).astype(BF16).astype(F32)
        code = (piece / scale).astype(BF16).astype(F32)
        return (scale * code).astype(BF16)

    peers = sorted(
        ((dy, dz) for dy in range(2) for dz in range(8) if dy or dz),
        key=lambda p_: -(p_[0] + min(p_[1], 8 - p_[1])),
    )

    def outer_send(m, buf, ss, rs):
        for dy, dz in peers:
            to = ((ylo + dy) % 2 * 8 + (z + dz) % 8, f)
            send(tb.at[m], buf.at[r], ss.at[0], rs.at[0], to)

    def outer_sum(m, buf, ss, rs):
        both(buf.at[pl.ds(0, 15)], ss.at[0], rs.at[0]).wait_recv()
        outer_o[m] = jnp.sum(buf[...].astype(F32), axis=0)

    piece = jnp.zeros((32, FRAG), F32)
    for b in range(C // FRAG):
        piece = jnp.where(chosen == b, gf[:, b * FRAG : (b + 1) * FRAG], piece)
    term = decoded(piece)
    tb[1] = term
    oo[r] = term
    outer_send(1, oo, s_oo, r_oo)

    msg_y(2)
    msg_y(3)
    msg_sum(0)
    term = decoded(jnp.where(chosen < 4, gm[0, 0], gm[1, 0]))
    tb[0] = term
    om[r] = term
    outer_send(0, om, s_om, r_om)
    arrived(part_r, s_misc.at[8], r_misc.at[8], partner)
    node_o[...] = (node_own + part_r[...].astype(F32)).astype(BF16)
    put(0, node_o, node_h)
    outer_sum(1, oo, s_oo, r_oo)
    for k in (1, 2, 3):
        msg_sum(k)
    for c_ in (0, 1):
        for k, v in enumerate(turned(32, True, lambda k: gm[c_, k])):
            gmsg_o[0, :, c_ * HC + k * FRAG : c_ * HC + (k + 1) * FRAG] = v.astype(BF16)
    put(1, gmsg_o, gmsg_h)
    outer_sum(0, om, s_om, r_om)
    put(3, outer_o, outer_h)

    for cp in puts:
        cp.wait()
    both(sm, s_xm.at[0], s_xm.at[0]).wait_send()
    both(idb.at[pl.ds(0, 3)], s_ix.at[0], r_ix.at[0]).wait_send()
    for k in range(4):
        both(ym.at[k, pl.ds(0, 7)], s_ym.at[k], r_ym.at[k]).wait_send()
    both(oo.at[pl.ds(0, 15)], s_oo.at[0], r_oo.at[0]).wait_send()
    both(om.at[pl.ds(0, 15)], s_om.at[0], r_om.at[0]).wait_send()
    for cp in sent:
        cp.wait_send()

    @pl.when(up_ok)
    def _():
        for c_ in (0, 1):
            up_copy(c_).wait_send()

    @pl.when(dn_ok)
    def _():
        for c_ in (0, 1):
            dn_copy(c_).wait_send()

    @pl.when(half != c)
    def _():
        wo_partner().wait_send()

    for n in (0, 1):
        both(wmb.at[0, pl.ds(0, 3)], s_wx.at[n], s_wx.at[n]).wait_send()
    both(wmb.at[0], s_wz.at[1], r_wz.at[1]).wait_send()

    for parity in (0, 1):
        @pl.when(par == parity)
        def _(parity=parity):
            for j in y_of[parity]:
                for c_ in (0, 1):
                    wm_y(j, c_).wait_send()
            ref = wmb.at[0] if parity else wmb.at[0, pl.ds(0, 3)]
            both(ref, s_wz.at[0], r_wz.at[0]).wait_send()

    @pl.when(h % 2 == par)
    def _():
        for j in range(3):
            wo_y(j).wait_send()

    @pl.when(h != 2 * c + par)
    def _():
        both(wob.at[0], s_oz.at[0], r_oz.at[0]).wait_send()

    @pl.when(h == 2 * c + par)
    def _():
        both(wob.at[0, pl.ds(0, 3)], s_oz.at[0], r_oz.at[0]).wait_send()
    @pl.when(q > 0)
    def _():
        rim_dn().wait_send()

    @pl.when(q < 15)
    def _():
        rim_up().wait_send()

    for e in (0, 1):
        for c_ in (0, 1):
            @pl.when(jnp.logical_not(jnp.logical_and(2 * c + e == h, c == c_)))
            def _(e=e, c_=c_):
                yo_copy(e, c_).wait_send()


def finish(*refs):
    sems = refs[8]
    copies = [pltpu.make_async_copy(refs[i], refs[4 + i], sems.at[i]) for i in range(4)]
    for cp in copies:
        cp.start()
    for cp in copies:
        cp.wait()


def shards(feats, src, dist, ids, wm, wo, radial, cot, frag):
    vm = pl.BlockSpec(memory_space=pltpu.VMEM)
    dma = lambda *n: pltpu.SemaphoreType.DMA(n)
    V = pltpu.VMEM
    results = pl.pallas_call(
        body,
        out_shape=(
            jax.ShapeDtypeStruct((A, C), BF16),
            jax.ShapeDtypeStruct((1, 32, C), BF16),
            jax.ShapeDtypeStruct((1, 32, C), BF16),
            jax.ShapeDtypeStruct((2, 32, FRAG), F32),
        ),
        in_specs=[pl.BlockSpec(memory_space=pl.ANY)] * 8 + [pl.BlockSpec(memory_space=pltpu.SMEM)],
        out_specs=(pl.BlockSpec(memory_space=pl.ANY),) * 4,
        scratch_shapes=[
            V((4, 4, 2, 32, HC), BF16),
            V((2, 4, 2, 32, C), BF16),
            V((32, C), BF16),
            V((32, C), BF16),
            V((BASIS, C), F32),
            V((4, 4, 2, 1, A), jnp.int32),
            V((EXT, C), BF16),
            V((2, A, C), BF16),
            V((2, NB, A), jnp.int32),
            V((2, NB, A), F32),
            V((A, C), BF16),
            V((H, HC), BF16),
            V((H, HC), BF16),
            V((6, 64, C), BF16),
            V((4, 6, A, FRAG), BF16),
            V((4, 32, C), BF16),
            V((4, 8, 32, FRAG), BF16),
            V((16, 32, FRAG), BF16),
            V((16, 32, FRAG), BF16),
            V((BASIS, NB, A), F32),
            V((BASIS * W, A), F32),
            V((2, W, BASIS * A), BF16),
            V((2, A, BASIS * W), BF16),
            V((BASIS * W, HC), BF16),
            V((2 * A, HC), BF16),
            V((2 * A, HC), F32),
            V((2, 4, 64, 2 * A), BF16),
            V((4, 4, 64, 2 * A), BF16),
            V((2 * A, C), BF16),
            V((BASIS * A, HC), BF16),
            V((EXT, HC), F32),
            V((2 * A, HC), BF16),
            V((A, C), BF16),
            V((2, H, HC), BF16),
            V((6, 64, C), BF16),
            V((4, 64, C), F32),
            V((4, 6, A, FRAG), BF16),
            V((4, 4, A, FRAG), F32),
            V((2, 2, 32, C), BF16),
            V((4, 4, 2, 32, FRAG), BF16),
            V((32, C), F32),
            V((2, 4, 32, FRAG), F32),
            V((2, 32, FRAG), BF16),
            V((A, C), BF16),
            V((1, 32, C), BF16),
            V((1, 32, C), BF16),
            V((2, 32, FRAG), F32),
            dma(14),
            dma(7), dma(7), dma(7), dma(7), dma(4), dma(7),
            dma(2), dma(2, 3), dma(2), dma(2), dma(1), dma(1),
            dma(4), dma(4), dma(1), dma(1),
            dma(9), dma(9), dma(6), dma(6), dma(1), dma(4, 2),
            dma(4), dma(4), dma(4), dma(4), dma(1), dma(1), dma(1), dma(1),
        ],
        compiler_params=pltpu.CompilerParams(
            collective_id=0, has_side_effects=True, vmem_limit_bytes=56 << 20
        ),
        name="step",
    )(feats, src, dist, ids, wm, wo, radial, cot, frag)
    anywhere = pl.BlockSpec(memory_space=pl.ANY)
    return pl.pallas_call(
        finish,
        out_shape=tuple(jax.ShapeDtypeStruct(v.shape, v.dtype) for v in results),
        in_specs=[vm] * 4,
        out_specs=(anywhere,) * 4,
        scratch_shapes=[dma(4)],
        compiler_params=pltpu.CompilerParams(vmem_limit_bytes=60 << 20),
        name="finish",
    )(*results)


def solution(mesh):
    placed = (
        P(("replica", "fsdp"), None),
        P(None, ("replica", "fsdp")),
        P(None, ("replica", "fsdp")),
        P("replica", "fsdp"),
        P("fsdp", None),
        P("fsdp", None),
        P(),
        P(("replica", "fsdp"), None),
        P(),
    )
    return jax.shard_map(
        shards,
        mesh=mesh,
        in_specs=placed,
        out_specs=(
            P(("replica", "fsdp"), None),
            P("replica", "fsdp", None),
            P("replica", "fsdp", None),
            P(None, "fsdp", None),
        ),
        check_vma=False,
    )
```
